256 devices in a mesh: expert: 64 (over y_hi, x, z), half: 2 (over y_lo), dp: 2 (over core).
Axes of the slice: x: 4, y: 4 (y_hi: 2, y_lo: 2; y = y_hi * 2 + y_lo), z: 8, core: 2. Of those that a mesh axis runs over, the one named last changes fastest.
Arguments:
- tokens: bfloat16 [16384, 4096], P(('expert', 'dp'), 'half'), may hold values from -6 to 6
- cotangent: bfloat16 [16384, 4096], P(('expert', 'dp'), 'half'), may hold values from -12 to 12
- expert_ids: int32 [16384, 8], P(('expert', 'dp')), may hold values from 0 to 63, as said below
- slot_ids: int32 [16384, 8], P(('expert', 'dp')), may hold values from 0 to 17, as said below
- gate_weights: float32 [16384, 8], P(('expert', 'dp')), may hold values from 0.03 to 0.4
- latent_down: bfloat16 [4096, 1024], P('half', 'dp'), may hold values from -0.09375 to 0.09375
- latent_up: bfloat16 [1024, 4096], P('dp', 'half'), may hold values from -0.1875 to 0.1875
- expert_gate: bfloat16 [64, 1024, 1536], P('expert', 'dp', 'half'), may hold values from -0.1875 to 0.1875
- expert_linear: bfloat16 [64, 1024, 1536], P('expert', 'dp', 'half'), may hold values from -0.1875 to 0.1875
- expert_out: bfloat16 [64, 1536, 1024], P('expert', 'half', 'dp'), may hold values from -0.15625 to 0.15625
Outputs:
- token_grad: bfloat16 [16384, 4096], P(('expert', 'dp'), 'half')
- gate_grad: bfloat16 [64, 1024, 1536], P('expert', 'dp', 'half')
- linear_grad: bfloat16 [64, 1024, 1536], P('expert', 'dp', 'half')
- out_grad: bfloat16 [64, 1536, 1024], P('expert', 'half', 'dp')
The draws below stay inside these ranges and needn't reach their ends.
Inputs may be any that keep to these rules, and one draw needn't show every extreme that they name: `expert_ids`: each row names 8 different experts. In each aligned block of 128 rows (the rows of one device) no expert is named by more than 18 rows, and one expert is named by exactly 18 rows in every block. `slot_ids`: within one aligned block of 128 rows, the entries that name the same expert have different slots.
All inputs are finite; a program needn't handle non-finite values.
Results may differ from the reference program's by a relative error of at most 0.013.
Values may be sent and summed in bfloat16 or wider, within the bound.
A program may use at most 128 MiB of HBM per device.

```python
import math
import jax
import jax.numpy as jnp
from jax import lax

D = 4096
LATENT = 1024
HIDDEN_SIZE = 1536
TOP = 8
TOK_DEV = 128
EXPERTS = 64
TOKENS = 16384
CAP = 18


def route_tables(key):
    blocks = TOKENS // TOK_DEV
    assigned = TOK_DEV * TOP
    even_load = assigned // EXPERTS
    remainder = assigned % EXPERTS
    ranking = jax.random.permutation(jax.random.fold_in(key, 101), EXPERTS).astype(jnp.int32)
    places = jnp.arange(EXPERTS, dtype=jnp.int32)
    counts = even_load + (places < remainder).astype(jnp.int32)
    first_loads = counts[0::2]
    second = counts[1::2]
    headroom = jnp.minimum(CAP - first_loads, second)
    pair_count = EXPERTS // 2
    limit = jnp.broadcast_to(headroom + 1, (blocks, pair_count))
    moved_loads = jax.random.randint(jax.random.fold_in(key, 102), (blocks, pair_count), 0, limit).astype(jnp.int32)
    moved_loads = moved_loads.at[:, 0].set(CAP - first_loads[0])
    block_loads = jnp.stack([first_loads[None, :] + moved_loads, second[None, :] - moved_loads], axis=2).reshape(blocks, EXPERTS)
    run_ends = jnp.cumsum(block_loads, axis=1)
    run_starts = run_ends - block_loads
    serial = jnp.arange(assigned, dtype=jnp.int32)
    run_index = jnp.sum((serial[None, :, None] >= run_ends[:, None, :]).astype(jnp.int32), axis=2)
    slot_table = serial[None, :] - jnp.take_along_axis(run_starts, run_index, axis=1)
    chosen = ranking[run_index]
    chosen = chosen.reshape(blocks, TOP, TOK_DEV).transpose(0, 2, 1)
    slot_table = slot_table.reshape(blocks, TOP, TOK_DEV).transpose(0, 2, 1)
    row_keys = jax.random.split(jax.random.fold_in(key, 103), blocks)
    shuffle = jax.vmap(lambda subkey: jax.random.permutation(subkey, TOK_DEV))(row_keys).astype(jnp.int32)
    chosen = jnp.take_along_axis(chosen, shuffle[:, :, None], axis=1)
    slot_table = jnp.take_along_axis(slot_table, shuffle[:, :, None], axis=1)
    rotate = jax.random.randint(jax.random.fold_in(key, 104), (blocks, TOK_DEV, 1), 0, TOP).astype(jnp.int32)
    column = (jnp.arange(TOP, dtype=jnp.int32)[None, None, :] + rotate) % TOP
    chosen = jnp.take_along_axis(chosen, column, axis=2)
    slot_table = jnp.take_along_axis(slot_table, column, axis=2)
    return (chosen.reshape(TOKENS, TOP).astype(jnp.int32), slot_table.reshape(TOKENS, TOP).astype(jnp.int32))


def draw_expert_ids(key, part):
    return route_tables(key)[0]


def draw_slot_ids(key, part):
    return route_tables(key)[1]


def shard_levels(key, shape, shards, least, high):
    loudness = 1.0
    for dim, blocks in shards:
        draws = jax.random.uniform(jax.random.fold_in(jax.random.fold_in(key, 6), dim), (blocks,), jnp.float32, least / len(shards), high / len(shards))
        loudness = loudness * jnp.repeat(jnp.exp(draws), shape[dim] // blocks).reshape((-1,) + (1,) * (len(shape) - 1 - dim))
    return loudness


def noise(key, shape, spread, most, shards=(), kind=jnp.bfloat16):
    loudness = shard_levels(key, shape, shards, -0.22, 0.18) if shards else 1.0
    result = jax.random.normal(key, shape, jnp.float32) * spread * loudness
    return jnp.minimum(jnp.maximum(result, -most), most).astype(kind)


def setup_inputs(seed: int = 0) -> dict:
    keys = jax.random.split(jax.random.key(seed), 11)
    return {
        "tokens": noise(keys[0], (TOKENS, D), 1.0, 6.0, ((0, 128), (1, 2))),
        "cotangent": noise(keys[1], (TOKENS, D), 2.0, 12.0, ((0, 128), (1, 2))),
        "expert_ids": draw_expert_ids(jax.random.fold_in(keys[10], 71), 0),
        "slot_ids": draw_slot_ids(jax.random.fold_in(keys[10], 71), 0),
        "gate_weights": jnp.clip(jnp.exp(math.log(0.4) - 2.5902672 * jax.random.uniform(keys[4], (TOKENS, TOP), jnp.float32) ** shard_levels(keys[4], (TOKENS, TOP), ((0, 128),), -0.2, 0.2)), 0.03, 0.4),
        "latent_down": noise(keys[5], (D, LATENT), D ** -0.5, 0.09375, ((0, 2), (1, 2))),
        "latent_up": noise(keys[6], (LATENT, D), LATENT ** -0.5, 0.1875, ((0, 2), (1, 2))),
        "expert_gate": noise(keys[7], (EXPERTS, LATENT, HIDDEN_SIZE), LATENT ** -0.5, 0.1875, ((0, 64), (1, 2), (2, 2))),
        "expert_linear": noise(keys[8], (EXPERTS, LATENT, HIDDEN_SIZE), LATENT ** -0.5, 0.1875, ((0, 64), (1, 2), (2, 2))),
        "expert_out": noise(keys[9], (EXPERTS, HIDDEN_SIZE, LATENT), HIDDEN_SIZE ** -0.5, 0.15625, ((0, 64), (1, 2), (2, 2))),
    }


def reference(tokens, cotangent, expert_ids, slot_ids, gate_weights, latent_down, latent_up, expert_gate, expert_linear, expert_out):
    latent = jnp.dot(tokens, latent_down, preferred_element_type=jnp.float32).astype(jnp.bfloat16)
    back_latent = lax.dot_general(cotangent, latent_up, (((1,), (1,)), ((), ())), preferred_element_type=jnp.float32)
    per_expert = (TOKENS // TOK_DEV) * CAP
    assigned = TOKENS * TOP
    token_index = jnp.arange(TOKENS, dtype=jnp.int32)
    block_of = token_index // TOK_DEV
    where_to = (expert_ids * per_expert + block_of[:, None] * CAP + slot_ids).astype(jnp.int32)
    sources = jnp.full((EXPERTS * per_expert,), assigned, jnp.int32)
    sources = sources.at[where_to.reshape(-1)].set(jnp.arange(assigned, dtype=jnp.int32))
    sources = sources.reshape(EXPERTS, per_expert)
    gate_flat = gate_weights.reshape(-1)

    def one_expert(operands):
        source_rows, w_gate, w_linear, w_out = operands
        filled = source_rows < assigned
        clamped = jnp.minimum(source_rows, assigned - 1)
        token_pos = clamped // TOP
        inputs = jnp.where(filled[:, None], latent[token_pos], jnp.zeros((), jnp.bfloat16))
        upstream = jnp.where(filled[:, None], gate_flat[clamped][:, None] * back_latent[token_pos], jnp.zeros((), jnp.float32)).astype(jnp.bfloat16)
        pre_gate = jnp.dot(inputs, w_gate, preferred_element_type=jnp.float32)
        pre_linear = jnp.dot(inputs, w_linear, preferred_element_type=jnp.float32)
        grad_hidden = lax.dot_general(upstream, w_out, (((1,), (1,)), ((), ())), preferred_element_type=jnp.float32)
        logistic = jax.nn.sigmoid(pre_gate)
        hidden = (pre_gate * logistic * pre_linear).astype(jnp.bfloat16)
        gate_delta = (grad_hidden * pre_linear * logistic * (1.0 + pre_gate * (1.0 - logistic))).astype(jnp.bfloat16)
        linear_delta = (grad_hidden * pre_gate * logistic).astype(jnp.bfloat16)
        grad_gate = lax.dot_general(inputs, gate_delta, (((0,), (0,)), ((), ())), preferred_element_type=jnp.float32)
        grad_linear = lax.dot_general(inputs, linear_delta, (((0,), (0,)), ((), ())), preferred_element_type=jnp.float32)
        grad_out = lax.dot_general(hidden, upstream, (((0,), (0,)), ((), ())), preferred_element_type=jnp.float32)
        row_grad = lax.dot_general(gate_delta, w_gate, (((1,), (1,)), ((), ())), preferred_element_type=jnp.float32)
        row_grad = row_grad + lax.dot_general(linear_delta, w_linear, (((1,), (1,)), ((), ())), preferred_element_type=jnp.float32)
        return grad_gate, grad_linear, grad_out, row_grad.astype(jnp.bfloat16)

    gate_grad, linear_grad, out_grad, row_grads = lax.map(one_expert, (sources, expert_gate, expert_linear, expert_out))
    picked = row_grads.reshape(EXPERTS * per_expert, LATENT)[where_to]
    latent_grad = jnp.sum(picked.astype(jnp.float32), axis=1).astype(jnp.bfloat16)
    token_grad = lax.dot_general(latent_grad, latent_down, (((1,), (1,)), ((), ())), preferred_element_type=jnp.float32)
    return token_grad.astype(jnp.bfloat16), gate_grad.astype(jnp.bfloat16), linear_grad.astype(jnp.bfloat16), out_grad.astype(jnp.bfloat16)
```

```python
import functools

import jax
import jax.numpy as jnp
from jax import lax
from jax.experimental import pallas as pl
from jax.experimental.pallas import tpu as pltpu
from jax.sharding import PartitionSpec as P

MESH = pl.DeviceIdType.MESH


def _pair_sum_kernel(x_ref, o_ref, buf, send_sem, recv_sem):
    other = 1 - lax.axis_index("half")
    barrier = pltpu.get_barrier_semaphore()
    pl.semaphore_signal(barrier, inc=1, device_id={"half": other}, device_id_type=MESH)
    pl.semaphore_wait(barrier, 1)
    copy = pltpu.make_async_remote_copy(
        src_ref=x_ref,
        dst_ref=buf,
        send_sem=send_sem,
        recv_sem=recv_sem,
        device_id={"half": other},
        device_id_type=MESH,
    )
    copy.start()
    copy.wait()
    o_ref[...] = x_ref[...] + buf[...]


def pair_sum(x, collective_id):
    return pl.pallas_call(
        _pair_sum_kernel,
        out_shape=jax.ShapeDtypeStruct(x.shape, x.dtype),
        in_specs=[pl.BlockSpec(memory_space=pltpu.VMEM)],
        out_specs=pl.BlockSpec(memory_space=pltpu.VMEM),
        scratch_shapes=[
            pltpu.VMEM(x.shape, x.dtype),
            pltpu.SemaphoreType.DMA(()),
            pltpu.SemaphoreType.DMA(()),
        ],
        compiler_params=pltpu.CompilerParams(collective_id=collective_id, has_side_effects=True),
    )(x)


def on_device(
    tokens,
    cotangent,
    expert_ids,
    slot_ids,
    gate_weights,
    latent_down,
    latent_up,
    expert_gate,
    expert_linear,
    expert_out,
):
    row_count = tokens.shape[0]
    pick_count = expert_ids.shape[1]
    local_count = expert_gate.shape[0]
    group_count = lax.axis_size("expert")
    expert_count = group_count * local_count
    capacity = min(
        row_count, 2 * ((9 * row_count * pick_count + 16 * expert_count - 1) // (16 * expert_count))
    )
    down_full, up_full, gate_full, linear_full, output_full = (
        lax.all_gather(latent_down, "dp", axis=1, tiled=True),
        lax.all_gather(latent_up, "dp", axis=0, tiled=True),
        lax.all_gather(expert_gate, "dp", axis=1, tiled=True),
        lax.all_gather(expert_linear, "dp", axis=1, tiled=True),
        lax.all_gather(expert_out, "dp", axis=2, tiled=True),
    )
    latent_part = jnp.dot(tokens, down_full, preferred_element_type=jnp.float32)
    back_part = lax.dot_general(
        cotangent, up_full, (((1,), (1,)), ((), ())), preferred_element_type=jnp.float32
    )
    width = latent_part.shape[1]
    both = pair_sum(jnp.concatenate([latent_part, back_part], axis=1), 1)
    latent = both[:, :width].astype(jnp.bfloat16)
    back_latent = both[:, width:]
    flat_slot = (expert_ids * capacity + slot_ids).reshape(-1)
    slot_table = lax.broadcasted_iota(
        jnp.int32, (expert_count * capacity, row_count * pick_count), 0
    )
    matches = flat_slot[None, :] == slot_table
    choice_index = lax.broadcasted_iota(jnp.int32, matches.shape, 1)
    source = jnp.sum(jnp.where(matches, choice_index, 0), axis=1)
    filled = jnp.any(matches, axis=1)
    token_of = source // pick_count
    gate_of = gate_weights.reshape(-1)[source]
    send_latent = jnp.where(filled[:, None], latent[token_of], jnp.zeros((), jnp.bfloat16))
    send_back = jnp.where(filled[:, None], gate_of[:, None] * back_latent[token_of], 0.0).astype(
        jnp.bfloat16
    )
    send = jnp.concatenate([send_latent, send_back], axis=1)
    send = send.reshape(group_count, local_count, capacity, 2 * width)
    rows = lax.all_to_all(send, "expert", split_axis=0, concat_axis=0, tiled=True)
    rows_latent = rows[..., :width]
    rows_back = rows[..., width:]
    pre_gate = jnp.einsum(
        "neci,eih->nech", rows_latent, gate_full, preferred_element_type=jnp.float32
    )
    pre_linear = jnp.einsum(
        "neci,eih->nech", rows_latent, linear_full, preferred_element_type=jnp.float32
    )
    grad_hidden = jnp.einsum(
        "necj,ehj->nech", rows_back, output_full, preferred_element_type=jnp.float32
    )
    logistic = jax.nn.sigmoid(pre_gate)
    hidden = (pre_gate * logistic * pre_linear).astype(jnp.bfloat16)
    gate_delta = (grad_hidden * pre_linear * logistic * (1.0 + pre_gate * (1.0 - logistic))).astype(
        jnp.bfloat16
    )
    linear_delta = (grad_hidden * pre_gate * logistic).astype(jnp.bfloat16)
    gate_part = jnp.einsum(
        "neci,nech->eih", rows_latent, gate_delta, preferred_element_type=jnp.float32
    )
    linear_part = jnp.einsum(
        "neci,nech->eih", rows_latent, linear_delta, preferred_element_type=jnp.float32
    )
    out_part = jnp.einsum("nech,necj->ehj", hidden, rows_back, preferred_element_type=jnp.float32)
    gate_share, linear_share, out_share = (
        lax.psum_scatter(
            gate_part.astype(jnp.bfloat16), "dp", scatter_dimension=1, tiled=True
        ).astype(jnp.float32),
        lax.psum_scatter(
            linear_part.astype(jnp.bfloat16), "dp", scatter_dimension=1, tiled=True
        ).astype(jnp.float32),
        lax.psum_scatter(
            out_part.astype(jnp.bfloat16), "dp", scatter_dimension=2, tiled=True
        ).astype(jnp.float32),
    )
    row_part = jnp.einsum(
        "nech,eih->neci", gate_delta, gate_full, preferred_element_type=jnp.float32
    )
    row_part = row_part + jnp.einsum(
        "nech,eih->neci", linear_delta, linear_full, preferred_element_type=jnp.float32
    )
    returned = lax.all_to_all(
        row_part.astype(jnp.bfloat16), "expert", split_axis=0, concat_axis=0, tiled=True
    )
    position = expert_ids * capacity + slot_ids
    gathered = returned.reshape(expert_count * capacity, width)[position]
    latent_half = jnp.sum(gathered.astype(jnp.float32), axis=1)
    latent_grad = pair_sum(latent_half, 2)
    token_grad = lax.dot_general(
        latent_grad.astype(jnp.bfloat16),
        down_full,
        (((1,), (1,)), ((), ())),
        preferred_element_type=jnp.float32,
    )
    return (
        token_grad.astype(jnp.bfloat16),
        gate_share.astype(jnp.bfloat16),
        linear_share.astype(jnp.bfloat16),
        out_share.astype(jnp.bfloat16),
    )


def solution(mesh):
    in_specs = (
        P(("expert", "dp"), "half"),
        P(("expert", "dp"), "half"),
        P(("expert", "dp"), None),
        P(("expert", "dp"), None),
        P(("expert", "dp"), None),
        P("half", "dp"),
        P("dp", "half"),
        P("expert", "dp", "half"),
        P("expert", "dp", "half"),
        P("expert", "half", "dp"),
    )
    out_specs = (
        P(("expert", "dp"), "half"),
        P("expert", "dp", "half"),
        P("expert", "dp", "half"),
        P("expert", "half", "dp"),
    )
    return jax.shard_map(
        on_device, mesh=mesh, in_specs=in_specs, out_specs=out_specs, check_vma=False
    )
```

```python
import functools

import jax
import jax.numpy as jnp
from jax import lax
from jax.experimental import pallas as pl
from jax.experimental.pallas import tpu as pltpu
from jax.sharding import PartitionSpec as P

MESH = pl.DeviceIdType.MESH


def _pair_sum_kernel(x_ref, o_ref, buf, send_sem, recv_sem):
    other = 1 - lax.axis_index("half")
    barrier = pltpu.get_barrier_semaphore()
    pl.semaphore_signal(barrier, inc=1, device_id={"half": other}, device_id_type=MESH)
    pl.semaphore_wait(barrier, 1)
    copy = pltpu.make_async_remote_copy(
        src_ref=x_ref,
        dst_ref=buf,
        send_sem=send_sem,
        recv_sem=recv_sem,
        device_id={"half": other},
        device_id_type=MESH,
    )
    copy.start()
    copy.wait()
    o_ref[...] = x_ref[...] + buf[...]


def pair_sum(x, collective_id):
    return pl.pallas_call(
        _pair_sum_kernel,
        out_shape=jax.ShapeDtypeStruct(x.shape, x.dtype),
        in_specs=[pl.BlockSpec(memory_space=pltpu.VMEM)],
        out_specs=pl.BlockSpec(memory_space=pltpu.VMEM),
        scratch_shapes=[
            pltpu.VMEM(x.shape, x.dtype),
            pltpu.SemaphoreType.DMA(()),
            pltpu.SemaphoreType.DMA(()),
        ],
        compiler_params=pltpu.CompilerParams(collective_id=collective_id, has_side_effects=True),
    )(x)


def _all_to_all_kernel(x_ref, o_ref, send_sem, recv_sem, local_sem):
    count = x_ref.shape[0]
    me = lax.axis_index("expert")
    barrier = pltpu.get_barrier_semaphore()

    def greet(step, carry):
        peer = lax.rem(me + step, count)
        pl.semaphore_signal(barrier, inc=1, device_id={"expert": peer}, device_id_type=MESH)
        return carry

    lax.fori_loop(1, count, greet, 0)
    pl.semaphore_wait(barrier, count - 1)
    local = pltpu.make_async_copy(x_ref.at[me], o_ref.at[me], local_sem)
    local.start()

    def remote(peer):
        return pltpu.make_async_remote_copy(
            src_ref=x_ref.at[peer],
            dst_ref=o_ref.at[me],
            send_sem=send_sem.at[peer],
            recv_sem=recv_sem.at[me],
            device_id={"expert": peer},
            device_id_type=MESH,
        )

    def send(step, carry):
        remote(lax.rem(me + step, count)).start()
        return carry

    lax.fori_loop(1, count, send, 0)

    def drain(step, carry):
        peer = lax.rem(me + step, count)
        remote(peer).wait_send()
        pltpu.make_async_remote_copy(
            src_ref=x_ref.at[peer],
            dst_ref=o_ref.at[peer],
            send_sem=send_sem.at[peer],
            recv_sem=recv_sem.at[peer],
            device_id={"expert": peer},
            device_id_type=MESH,
        ).wait_recv()
        return carry

    lax.fori_loop(1, count, drain, 0)
    local.wait()


def all_to_all_kernel(x, collective_id):
    count = lax.axis_size("expert")
    shape = x.shape
    blocks = x.reshape(count, -1, shape[-1])
    out = pl.pallas_call(
        _all_to_all_kernel,
        out_shape=jax.ShapeDtypeStruct(blocks.shape, blocks.dtype),
        in_specs=[pl.BlockSpec(memory_space=pl.ANY)],
        out_specs=pl.BlockSpec(memory_space=pl.ANY),
        scratch_shapes=[
            pltpu.SemaphoreType.DMA((count,)),
            pltpu.SemaphoreType.DMA((count,)),
            pltpu.SemaphoreType.DMA(()),
        ],
        compiler_params=pltpu.CompilerParams(collective_id=collective_id, has_side_effects=True),
    )(blocks)
    return out.reshape(shape)


def on_device(
    tokens,
    cotangent,
    expert_ids,
    slot_ids,
    gate_weights,
    latent_down,
    latent_up,
    expert_gate,
    expert_linear,
    expert_out,
):
    row_count = tokens.shape[0]
    pick_count = expert_ids.shape[1]
    local_count = expert_gate.shape[0]
    group_count = lax.axis_size("expert")
    expert_count = group_count * local_count
    capacity = min(
        row_count, 2 * ((9 * row_count * pick_count + 16 * expert_count - 1) // (16 * expert_count))
    )
    down_full, up_full, gate_full, linear_full, output_full = (
        lax.all_gather(latent_down, "dp", axis=1, tiled=True),
        lax.all_gather(latent_up, "dp", axis=0, tiled=True),
        lax.all_gather(expert_gate, "dp", axis=1, tiled=True),
        lax.all_gather(expert_linear, "dp", axis=1, tiled=True),
        lax.all_gather(expert_out, "dp", axis=2, tiled=True),
    )
    latent_part = jnp.dot(tokens, down_full, preferred_element_type=jnp.float32)
    back_part = lax.dot_general(
        cotangent, up_full, (((1,), (1,)), ((), ())), preferred_element_type=jnp.float32
    )
    width = latent_part.shape[1]
    both = pair_sum(jnp.concatenate([latent_part, back_part], axis=1), 1)
    latent = both[:, :width].astype(jnp.bfloat16)
    back_latent = both[:, width:]
    flat_slot = (expert_ids * capacity + slot_ids).reshape(-1)
    slot_table = lax.broadcasted_iota(
        jnp.int32, (expert_count * capacity, row_count * pick_count), 0
    )
    matches = flat_slot[None, :] == slot_table
    choice_index = lax.broadcasted_iota(jnp.int32, matches.shape, 1)
    source = jnp.sum(jnp.where(matches, choice_index, 0), axis=1)
    filled = jnp.any(matches, axis=1)
    token_of = source // pick_count
    gate_of = gate_weights.reshape(-1)[source]
    send_latent = jnp.where(filled[:, None], latent[token_of], jnp.zeros((), jnp.bfloat16))
    send_back = jnp.where(filled[:, None], gate_of[:, None] * back_latent[token_of], 0.0).astype(
        jnp.bfloat16
    )
    send = jnp.concatenate([send_latent, send_back], axis=1)
    send = send.reshape(group_count, local_count, capacity, 2 * width)
    rows = all_to_all_kernel(send, 3)
    rows_latent = rows[..., :width]
    rows_back = rows[..., width:]
    pre_gate = jnp.einsum(
        "neci,eih->nech", rows_latent, gate_full, preferred_element_type=jnp.float32
    )
    pre_linear = jnp.einsum(
        "neci,eih->nech", rows_latent, linear_full, preferred_element_type=jnp.float32
    )
    grad_hidden = jnp.einsum(
        "necj,ehj->nech", rows_back, output_full, preferred_element_type=jnp.float32
    )
    logistic = jax.nn.sigmoid(pre_gate)
    hidden = (pre_gate * logistic * pre_linear).astype(jnp.bfloat16)
    gate_delta = (grad_hidden * pre_linear * logistic * (1.0 + pre_gate * (1.0 - logistic))).astype(
        jnp.bfloat16
    )
    linear_delta = (grad_hidden * pre_gate * logistic).astype(jnp.bfloat16)
    gate_part = jnp.einsum(
        "neci,nech->eih", rows_latent, gate_delta, preferred_element_type=jnp.float32
    )
    linear_part = jnp.einsum(
        "neci,nech->eih", rows_latent, linear_delta, preferred_element_type=jnp.float32
    )
    out_part = jnp.einsum("nech,necj->ehj", hidden, rows_back, preferred_element_type=jnp.float32)
    gate_share, linear_share, out_share = (
        lax.psum_scatter(
            gate_part.astype(jnp.bfloat16), "dp", scatter_dimension=1, tiled=True
        ).astype(jnp.float32),
        lax.psum_scatter(
            linear_part.astype(jnp.bfloat16), "dp", scatter_dimension=1, tiled=True
        ).astype(jnp.float32),
        lax.psum_scatter(
            out_part.astype(jnp.bfloat16), "dp", scatter_dimension=2, tiled=True
        ).astype(jnp.float32),
    )
    row_part = jnp.einsum(
        "nech,eih->neci", gate_delta, gate_full, preferred_element_type=jnp.float32
    )
    row_part = row_part + jnp.einsum(
        "nech,eih->neci", linear_delta, linear_full, preferred_element_type=jnp.float32
    )
    returned = all_to_all_kernel(row_part.astype(jnp.bfloat16), 4)
    position = expert_ids * capacity + slot_ids
    gathered = returned.reshape(expert_count * capacity, width)[position]
    latent_half = jnp.sum(gathered.astype(jnp.float32), axis=1)
    latent_grad = pair_sum(latent_half, 2)
    token_grad = lax.dot_general(
        latent_grad.astype(jnp.bfloat16),
        down_full,
        (((1,), (1,)), ((), ())),
        preferred_element_type=jnp.float32,
    )
    return (
        token_grad.astype(jnp.bfloat16),
        gate_share.astype(jnp.bfloat16),
        linear_share.astype(jnp.bfloat16),
        out_share.astype(jnp.bfloat16),
    )


def solution(mesh):
    in_specs = (
        P(("expert", "dp"), "half"),
        P(("expert", "dp"), "half"),
        P(("expert", "dp"), None),
        P(("expert", "dp"), None),
        P(("expert", "dp"), None),
        P("half", "dp"),
        P("dp", "half"),
        P("expert", "dp", "half"),
        P("expert", "dp", "half"),
        P("expert", "half", "dp"),
    )
    out_specs = (
        P(("expert", "dp"), "half"),
        P("expert", "dp", "half"),
        P("expert", "dp", "half"),
        P("expert", "half", "dp"),
    )
    return jax.shard_map(
        on_device, mesh=mesh, in_specs=in_specs, out_specs=out_specs, check_vma=False
    )
```

```python
import functools

import jax
import jax.numpy as jnp
from jax import lax
from jax.experimental import pallas as pl
from jax.experimental.pallas import tpu as pltpu
from jax.sharding import PartitionSpec as P

MESH = pl.DeviceIdType.MESH


def _pair_sum_kernel(x_ref, o_ref, buf, send_sem, recv_sem):
    other = 1 - lax.axis_index("half")
    barrier = pltpu.get_barrier_semaphore()
    pl.semaphore_signal(barrier, inc=1, device_id={"half": other}, device_id_type=MESH)
    pl.semaphore_wait(barrier, 1)
    copy = pltpu.make_async_remote_copy(
        src_ref=x_ref,
        dst_ref=buf,
        send_sem=send_sem,
        recv_sem=recv_sem,
        device_id={"half": other},
        device_id_type=MESH,
    )
    copy.start()
    copy.wait()
    o_ref[...] = x_ref[...] + buf[...]


def pair_sum(x, collective_id):
    return pl.pallas_call(
        _pair_sum_kernel,
        out_shape=jax.ShapeDtypeStruct(x.shape, x.dtype),
        in_specs=[pl.BlockSpec(memory_space=pltpu.VMEM)],
        out_specs=pl.BlockSpec(memory_space=pltpu.VMEM),
        scratch_shapes=[
            pltpu.VMEM(x.shape, x.dtype),
            pltpu.SemaphoreType.DMA(()),
            pltpu.SemaphoreType.DMA(()),
        ],
        compiler_params=pltpu.CompilerParams(collective_id=collective_id, has_side_effects=True),
    )(x)


def _all_to_all_kernel(x_ref, o_ref, send_sem, recv_sem, local_sem):
    count = x_ref.shape[0]
    me = lax.axis_index("expert")
    barrier = pltpu.get_barrier_semaphore()

    def greet(step, carry):
        peer = lax.rem(me + step, count)
        pl.semaphore_signal(barrier, inc=1, device_id={"expert": peer}, device_id_type=MESH)
        return carry

    lax.fori_loop(1, count, greet, 0)
    pl.semaphore_wait(barrier, count - 1)
    local = pltpu.make_async_copy(x_ref.at[me], o_ref.at[me], local_sem)
    local.start()

    def remote(peer):
        return pltpu.make_async_remote_copy(
            src_ref=x_ref.at[peer],
            dst_ref=o_ref.at[me],
            send_sem=send_sem.at[peer],
            recv_sem=recv_sem.at[me],
            device_id={"expert": peer},
            device_id_type=MESH,
        )

    def send(step, carry):
        remote(lax.rem(me + step, count)).start()
        return carry

    lax.fori_loop(1, count, send, 0)

    def drain(step, carry):
        peer = lax.rem(me + step, count)
        remote(peer).wait_send()
        pltpu.make_async_remote_copy(
            src_ref=x_ref.at[peer],
            dst_ref=o_ref.at[peer],
            send_sem=send_sem.at[peer],
            recv_sem=recv_sem.at[peer],
            device_id={"expert": peer},
            device_id_type=MESH,
        ).wait_recv()
        return carry

    lax.fori_loop(1, count, drain, 0)
    local.wait()


def all_to_all_kernel(x, collective_id):
    count = lax.axis_size("expert")
    shape = x.shape
    blocks = x.reshape(count, -1, shape[-1])
    out = pl.pallas_call(
        _all_to_all_kernel,
        out_shape=jax.ShapeDtypeStruct(blocks.shape, blocks.dtype),
        in_specs=[pl.BlockSpec(memory_space=pl.ANY)],
        out_specs=pl.BlockSpec(memory_space=pl.ANY),
        scratch_shapes=[
            pltpu.SemaphoreType.DMA((count,)),
            pltpu.SemaphoreType.DMA((count,)),
            pltpu.SemaphoreType.DMA(()),
        ],
        compiler_params=pltpu.CompilerParams(collective_id=collective_id, has_side_effects=True),
    )(blocks)
    return out.reshape(shape)


def on_device(
    tokens,
    cotangent,
    expert_ids,
    slot_ids,
    gate_weights,
    latent_down,
    latent_up,
    expert_gate,
    expert_linear,
    expert_out,
):
    row_count = tokens.shape[0]
    pick_count = expert_ids.shape[1]
    local_count = expert_gate.shape[0]
    group_count = lax.axis_size("expert")
    expert_count = group_count * local_count
    capacity = min(
        row_count, 2 * ((9 * row_count * pick_count + 16 * expert_count - 1) // (16 * expert_count))
    )
    down_full, up_full, gate_full, linear_full, output_full = (
        lax.all_gather(latent_down, "dp", axis=1, tiled=True),
        lax.all_gather(latent_up, "dp", axis=0, tiled=True),
        lax.all_gather(expert_gate, "dp", axis=1, tiled=True),
        lax.all_gather(expert_linear, "dp", axis=1, tiled=True),
        lax.all_gather(expert_out, "dp", axis=2, tiled=True),
    )
    latent_part = jnp.dot(tokens, down_full, preferred_element_type=jnp.float32)
    back_part = lax.dot_general(
        cotangent, up_full, (((1,), (1,)), ((), ())), preferred_element_type=jnp.float32
    )
    width = latent_part.shape[1]
    both = pair_sum(jnp.concatenate([latent_part, back_part], axis=1), 1)
    latent = both[:, :width].astype(jnp.bfloat16)
    back_latent = both[:, width:]
    half_cap = capacity // 2
    side = lax.axis_index("half")
    swap = [(0, 1), (1, 0)]
    flat_slot = (expert_ids * capacity + slot_ids).reshape(-1)
    owned_shape = (expert_count, half_cap)
    owned_slot = (
        lax.broadcasted_iota(jnp.int32, owned_shape, 0) * capacity
        + side * half_cap
        + lax.broadcasted_iota(jnp.int32, owned_shape, 1)
    ).reshape(-1)
    matches = flat_slot[None, :] == owned_slot[:, None]
    choice_index = lax.broadcasted_iota(jnp.int32, matches.shape, 1)
    source = jnp.sum(jnp.where(matches, choice_index, 0), axis=1)
    filled = jnp.any(matches, axis=1)
    token_of = source // pick_count
    gate_of = gate_weights.reshape(-1)[source]
    send_latent = jnp.where(filled[:, None], latent[token_of], jnp.zeros((), jnp.bfloat16))
    send_back = jnp.where(filled[:, None], gate_of[:, None] * back_latent[token_of], 0.0).astype(
        jnp.bfloat16
    )
    send = jnp.concatenate([send_latent, send_back], axis=1)
    send = send.reshape(group_count, local_count, half_cap, 2 * width)
    mine = all_to_all_kernel(send, 3)
    theirs = lax.ppermute(mine, "half", swap)

    def forward(rows):
        rows_latent = rows[..., :width]
        rows_back = rows[..., width:]
        pre_gate = jnp.einsum(
            "neci,eih->nech", rows_latent, gate_full, preferred_element_type=jnp.float32
        )
        pre_linear = jnp.einsum(
            "neci,eih->nech", rows_latent, linear_full, preferred_element_type=jnp.float32
        )
        grad_hidden = jnp.einsum(
            "necj,ehj->nech", rows_back, output_full, preferred_element_type=jnp.float32
        )
        logistic = jax.nn.sigmoid(pre_gate)
        hidden = (pre_gate * logistic * pre_linear).astype(jnp.bfloat16)
        gate_delta = (
            grad_hidden * pre_linear * logistic * (1.0 + pre_gate * (1.0 - logistic))
        ).astype(jnp.bfloat16)
        linear_delta = (grad_hidden * pre_gate * logistic).astype(jnp.bfloat16)
        return rows_latent, rows_back, hidden, gate_delta, linear_delta

    def row_grad(gate_delta, linear_delta):
        row_part = jnp.einsum(
            "nech,eih->neci", gate_delta, gate_full, preferred_element_type=jnp.float32
        )
        return row_part + jnp.einsum(
            "nech,eih->neci", linear_delta, linear_full, preferred_element_type=jnp.float32
        )

    def weight_grads(rows_latent, rows_back, hidden, gate_delta, linear_delta):
        gate_part = jnp.einsum(
            "neci,nech->eih", rows_latent, gate_delta, preferred_element_type=jnp.float32
        )
        linear_part = jnp.einsum(
            "neci,nech->eih", rows_latent, linear_delta, preferred_element_type=jnp.float32
        )
        out_part = jnp.einsum(
            "nech,necj->ehj", hidden, rows_back, preferred_element_type=jnp.float32
        )
        return gate_part, linear_part, out_part

    own = forward(mine)
    other = forward(theirs)
    other_rows = lax.ppermute(row_grad(other[3], other[4]).astype(jnp.bfloat16), "half", swap)
    own_rows = row_grad(own[3], own[4]) + other_rows.astype(jnp.float32)
    own_parts = weight_grads(*own)
    other_parts = weight_grads(*other)
    gate_part, linear_part, out_part = (a + b for a, b in zip(own_parts, other_parts))
    gate_share, linear_share, out_share = (
        lax.psum_scatter(
            gate_part.astype(jnp.bfloat16), "dp", scatter_dimension=1, tiled=True
        ).astype(jnp.float32),
        lax.psum_scatter(
            linear_part.astype(jnp.bfloat16), "dp", scatter_dimension=1, tiled=True
        ).astype(jnp.float32),
        lax.psum_scatter(
            out_part.astype(jnp.bfloat16), "dp", scatter_dimension=2, tiled=True
        ).astype(jnp.float32),
    )
    returned = all_to_all_kernel(own_rows.astype(jnp.bfloat16), 4)
    slot_rel = slot_ids - side * half_cap
    owned = (slot_rel >= 0) & (slot_rel < half_cap)
    position = expert_ids * half_cap + jnp.clip(slot_rel, 0, half_cap - 1)
    gathered = returned.reshape(expert_count * half_cap, width)[position]
    latent_half = jnp.sum(jnp.where(owned[..., None], gathered.astype(jnp.float32), 0.0), axis=1)
    latent_grad = pair_sum(latent_half, 2)
    token_grad = lax.dot_general(
        latent_grad.astype(jnp.bfloat16),
        down_full,
        (((1,), (1,)), ((), ())),
        preferred_element_type=jnp.float32,
    )
    return (
        token_grad.astype(jnp.bfloat16),
        gate_share.astype(jnp.bfloat16),
        linear_share.astype(jnp.bfloat16),
        out_share.astype(jnp.bfloat16),
    )


def solution(mesh):
    in_specs = (
        P(("expert", "dp"), "half"),
        P(("expert", "dp"), "half"),
        P(("expert", "dp"), None),
        P(("expert", "dp"), None),
        P(("expert", "dp"), None),
        P("half", "dp"),
        P("dp", "half"),
        P("expert", "dp", "half"),
        P("expert", "dp", "half"),
        P("expert", "half", "dp"),
    )
    out_specs = (
        P(("expert", "dp"), "half"),
        P("expert", "dp", "half"),
        P("expert", "dp", "half"),
        P("expert", "half", "dp"),
    )
    return jax.shard_map(
        on_device, mesh=mesh, in_specs=in_specs, out_specs=out_specs, check_vma=False
    )
```

```python
import functools

import jax
import jax.numpy as jnp
from jax import lax
from jax.experimental import pallas as pl
from jax.experimental.pallas import tpu as pltpu
from jax.sharding import PartitionSpec as P

MESH = pl.DeviceIdType.MESH


def _pair_sum_kernel(x_ref, o_ref, buf, send_sem, recv_sem):
    other = 1 - lax.axis_index("half")
    barrier = pltpu.get_barrier_semaphore()
    pl.semaphore_signal(barrier, inc=1, device_id={"half": other}, device_id_type=MESH)
    pl.semaphore_wait(barrier, 1)
    copy = pltpu.make_async_remote_copy(
        src_ref=x_ref,
        dst_ref=buf,
        send_sem=send_sem,
        recv_sem=recv_sem,
        device_id={"half": other},
        device_id_type=MESH,
    )
    copy.start()
    copy.wait()
    o_ref[...] = x_ref[...].astype(jnp.float32) + buf[...].astype(jnp.float32)


def pair_sum(x, collective_id):
    x = x.astype(jnp.bfloat16)
    return pl.pallas_call(
        _pair_sum_kernel,
        out_shape=jax.ShapeDtypeStruct(x.shape, jnp.float32),
        in_specs=[pl.BlockSpec(memory_space=pltpu.VMEM)],
        out_specs=pl.BlockSpec(memory_space=pltpu.VMEM),
        scratch_shapes=[
            pltpu.VMEM(x.shape, x.dtype),
            pltpu.SemaphoreType.DMA(()),
            pltpu.SemaphoreType.DMA(()),
        ],
        compiler_params=pltpu.CompilerParams(collective_id=collective_id, has_side_effects=True),
    )(x)


def _all_to_all_kernel(x_ref, o_ref, send_sem, recv_sem, local_sem):
    count = x_ref.shape[0]
    me = lax.axis_index("expert")
    barrier = pltpu.get_barrier_semaphore()

    def greet(step, carry):
        peer = lax.rem(me + step, count)
        pl.semaphore_signal(barrier, inc=1, device_id={"expert": peer}, device_id_type=MESH)
        return carry

    lax.fori_loop(1, count, greet, 0)
    pl.semaphore_wait(barrier, count - 1)
    local = pltpu.make_async_copy(x_ref.at[me], o_ref.at[me], local_sem)
    local.start()

    def remote(peer):
        return pltpu.make_async_remote_copy(
            src_ref=x_ref.at[peer],
            dst_ref=o_ref.at[me],
            send_sem=send_sem.at[peer],
            recv_sem=recv_sem.at[me],
            device_id={"expert": peer},
            device_id_type=MESH,
        )

    def send(step, carry):
        remote(lax.rem(me + step, count)).start()
        return carry

    lax.fori_loop(1, count, send, 0)

    def drain(step, carry):
        peer = lax.rem(me + step, count)
        remote(peer).wait_send()
        pltpu.make_async_remote_copy(
            src_ref=x_ref.at[peer],
            dst_ref=o_ref.at[peer],
            send_sem=send_sem.at[peer],
            recv_sem=recv_sem.at[peer],
            device_id={"expert": peer},
            device_id_type=MESH,
        ).wait_recv()
        return carry

    lax.fori_loop(1, count, drain, 0)
    local.wait()


def all_to_all_kernel(x, collective_id):
    count = lax.axis_size("expert")
    shape = x.shape
    blocks = x.reshape(count, -1, shape[-1])
    out = pl.pallas_call(
        _all_to_all_kernel,
        out_shape=jax.ShapeDtypeStruct(blocks.shape, blocks.dtype),
        in_specs=[pl.BlockSpec(memory_space=pl.ANY)],
        out_specs=pl.BlockSpec(memory_space=pl.ANY),
        scratch_shapes=[
            pltpu.SemaphoreType.DMA((count,)),
            pltpu.SemaphoreType.DMA((count,)),
            pltpu.SemaphoreType.DMA(()),
        ],
        compiler_params=pltpu.CompilerParams(collective_id=collective_id, has_side_effects=True),
    )(blocks)
    return out.reshape(shape)


def on_device(
    tokens,
    cotangent,
    expert_ids,
    slot_ids,
    gate_weights,
    latent_down,
    latent_up,
    expert_gate,
    expert_linear,
    expert_out,
):
    row_count = tokens.shape[0]
    pick_count = expert_ids.shape[1]
    local_count = expert_gate.shape[0]
    group_count = lax.axis_size("expert")
    expert_count = group_count * local_count
    capacity = min(
        row_count, 2 * ((9 * row_count * pick_count + 16 * expert_count - 1) // (16 * expert_count))
    )
    down_full, up_full, gate_full, linear_full, output_full = (
        lax.all_gather(latent_down, "dp", axis=1, tiled=True),
        lax.all_gather(latent_up, "dp", axis=0, tiled=True),
        lax.all_gather(expert_gate, "dp", axis=1, tiled=True),
        lax.all_gather(expert_linear, "dp", axis=1, tiled=True),
        lax.all_gather(expert_out, "dp", axis=2, tiled=True),
    )
    latent_part = jnp.dot(tokens, down_full, preferred_element_type=jnp.float32)
    back_part = lax.dot_general(
        cotangent, up_full, (((1,), (1,)), ((), ())), preferred_element_type=jnp.float32
    )
    width = latent_part.shape[1]
    both = pair_sum(jnp.concatenate([latent_part, back_part], axis=1), 1)
    latent = both[:, :width].astype(jnp.bfloat16)
    back_latent = both[:, width:]
    half_cap = capacity // 2
    side = lax.axis_index("half")
    swap = [(0, 1), (1, 0)]
    flat_slot = (expert_ids * capacity + slot_ids).reshape(-1)
    owned_shape = (expert_count, half_cap)
    owned_slot = (
        lax.broadcasted_iota(jnp.int32, owned_shape, 0) * capacity
        + side * half_cap
        + lax.broadcasted_iota(jnp.int32, owned_shape, 1)
    ).reshape(-1)
    matches = flat_slot[None, :] == owned_slot[:, None]
    choice_index = lax.broadcasted_iota(jnp.int32, matches.shape, 1)
    source = jnp.sum(jnp.where(matches, choice_index, 0), axis=1)
    filled = jnp.any(matches, axis=1)
    token_of = source // pick_count
    gate_of = gate_weights.reshape(-1)[source]
    send_latent = jnp.where(filled[:, None], latent[token_of], jnp.zeros((), jnp.bfloat16))
    send_back = jnp.where(filled[:, None], gate_of[:, None] * back_latent[token_of], 0.0).astype(
        jnp.bfloat16
    )
    send = jnp.concatenate([send_latent, send_back], axis=1)
    send = send.reshape(group_count, local_count, half_cap, 2 * width)
    mine = all_to_all_kernel(send, 3)
    theirs = lax.ppermute(mine, "half", swap)

    def forward(rows):
        rows_latent = rows[..., :width]
        rows_back = rows[..., width:]
        pre_gate = jnp.einsum(
            "neci,eih->nech", rows_latent, gate_full, preferred_element_type=jnp.float32
        )
        pre_linear = jnp.einsum(
            "neci,eih->nech", rows_latent, linear_full, preferred_element_type=jnp.float32
        )
        grad_hidden = jnp.einsum(
            "necj,ehj->nech", rows_back, output_full, preferred_element_type=jnp.float32
        )
        logistic = jax.nn.sigmoid(pre_gate)
        hidden = (pre_gate * logistic * pre_linear).astype(jnp.bfloat16)
        gate_delta = (
            grad_hidden * pre_linear * logistic * (1.0 + pre_gate * (1.0 - logistic))
        ).astype(jnp.bfloat16)
        linear_delta = (grad_hidden * pre_gate * logistic).astype(jnp.bfloat16)
        return rows_latent, rows_back, hidden, gate_delta, linear_delta

    def row_grad(gate_delta, linear_delta):
        row_part = jnp.einsum(
            "nech,eih->neci", gate_delta, gate_full, preferred_element_type=jnp.float32
        )
        return row_part + jnp.einsum(
            "nech,eih->neci", linear_delta, linear_full, preferred_element_type=jnp.float32
        )

    def weight_grads(rows_latent, rows_back, hidden, gate_delta, linear_delta):
        gate_part = jnp.einsum(
            "neci,nech->eih", rows_latent, gate_delta, preferred_element_type=jnp.float32
        )
        linear_part = jnp.einsum(
            "neci,nech->eih", rows_latent, linear_delta, preferred_element_type=jnp.float32
        )
        out_part = jnp.einsum(
            "nech,necj->ehj", hidden, rows_back, preferred_element_type=jnp.float32
        )
        return gate_part, linear_part, out_part

    own = forward(mine)
    own_row = row_grad(own[3], own[4])
    own_parts = weight_grads(*own)
    theirs, own_row, own_parts = lax.optimization_barrier((theirs, own_row, own_parts))
    other = forward(theirs)
    send_rows = row_grad(other[3], other[4]).astype(jnp.bfloat16)
    send_rows, other = lax.optimization_barrier((send_rows, other))
    other_rows = lax.ppermute(send_rows, "half", swap)
    other_parts = weight_grads(*other)
    other_rows, other_parts = lax.optimization_barrier((other_rows, other_parts))
    own_rows = own_row + other_rows.astype(jnp.float32)
    gate_part, linear_part, out_part = (a + b for a, b in zip(own_parts, other_parts))
    gate_share, linear_share, out_share = (
        lax.psum_scatter(
            gate_part.astype(jnp.bfloat16), "dp", scatter_dimension=1, tiled=True
        ).astype(jnp.float32),
        lax.psum_scatter(
            linear_part.astype(jnp.bfloat16), "dp", scatter_dimension=1, tiled=True
        ).astype(jnp.float32),
        lax.psum_scatter(
            out_part.astype(jnp.bfloat16), "dp", scatter_dimension=2, tiled=True
        ).astype(jnp.float32),
    )
    returned = all_to_all_kernel(own_rows.astype(jnp.bfloat16), 4)
    slot_rel = slot_ids - side * half_cap
    owned = (slot_rel >= 0) & (slot_rel < half_cap)
    position = expert_ids * half_cap + jnp.clip(slot_rel, 0, half_cap - 1)
    gathered = returned.reshape(expert_count * half_cap, width)[position]
    latent_half = jnp.sum(jnp.where(owned[..., None], gathered.astype(jnp.float32), 0.0), axis=1)
    latent_grad = pair_sum(latent_half, 2)
    token_grad = lax.dot_general(
        latent_grad.astype(jnp.bfloat16),
        down_full,
        (((1,), (1,)), ((), ())),
        preferred_element_type=jnp.float32,
    )
    return (
        token_grad.astype(jnp.bfloat16),
        gate_share.astype(jnp.bfloat16),
        linear_share.astype(jnp.bfloat16),
        out_share.astype(jnp.bfloat16),
    )


def solution(mesh):
    in_specs = (
        P(("expert", "dp"), "half"),
        P(("expert", "dp"), "half"),
        P(("expert", "dp"), None),
        P(("expert", "dp"), None),
        P(("expert", "dp"), None),
        P("half", "dp"),
        P("dp", "half"),
        P("expert", "dp", "half"),
        P("expert", "dp", "half"),
        P("expert", "half", "dp"),
    )
    out_specs = (
        P(("expert", "dp"), "half"),
        P("expert", "dp", "half"),
        P("expert", "dp", "half"),
        P("expert", "half", "dp"),
    )
    return jax.shard_map(
        on_device, mesh=mesh, in_specs=in_specs, out_specs=out_specs, check_vma=False
    )
```

```python
import functools

import jax
import jax.numpy as jnp
from jax import lax
from jax.experimental import pallas as pl
from jax.experimental.pallas import tpu as pltpu
from jax.sharding import PartitionSpec as P

MESH = pl.DeviceIdType.MESH


def _pair_sum_kernel(x_ref, o_ref, buf, send_sem, recv_sem):
    other = 1 - lax.axis_index("half")
    barrier = pltpu.get_barrier_semaphore()
    pl.semaphore_signal(barrier, inc=1, device_id={"half": other}, device_id_type=MESH)
    pl.semaphore_wait(barrier, 1)
    copy = pltpu.make_async_remote_copy(
        src_ref=x_ref,
        dst_ref=buf,
        send_sem=send_sem,
        recv_sem=recv_sem,
        device_id={"half": other},
        device_id_type=MESH,
    )
    copy.start()
    copy.wait()
    o_ref[...] = x_ref[...].astype(jnp.float32) + buf[...].astype(jnp.float32)


def pair_sum(x, collective_id):
    x = x.astype(jnp.bfloat16)
    return pl.pallas_call(
        _pair_sum_kernel,
        out_shape=jax.ShapeDtypeStruct(x.shape, jnp.float32),
        in_specs=[pl.BlockSpec(memory_space=pltpu.VMEM)],
        out_specs=pl.BlockSpec(memory_space=pltpu.VMEM),
        scratch_shapes=[
            pltpu.VMEM(x.shape, x.dtype),
            pltpu.SemaphoreType.DMA(()),
            pltpu.SemaphoreType.DMA(()),
        ],
        compiler_params=pltpu.CompilerParams(collective_id=collective_id, has_side_effects=True),
    )(x)


def _all_to_all_kernel(x_ref, o_ref, send_sem, recv_sem, local_sem):
    count = x_ref.shape[0]
    me = lax.axis_index("expert")
    barrier = pltpu.get_barrier_semaphore()

    def greet(step, carry):
        peer = lax.rem(me + step, count)
        pl.semaphore_signal(barrier, inc=1, device_id={"expert": peer}, device_id_type=MESH)
        return carry

    lax.fori_loop(1, count, greet, 0)
    pl.semaphore_wait(barrier, count - 1)
    local = pltpu.make_async_copy(x_ref.at[me], o_ref.at[me], local_sem)
    local.start()

    def remote(peer):
        return pltpu.make_async_remote_copy(
            src_ref=x_ref.at[peer],
            dst_ref=o_ref.at[me],
            send_sem=send_sem.at[peer],
            recv_sem=recv_sem.at[me],
            device_id={"expert": peer},
            device_id_type=MESH,
        )

    def send(step, carry):
        remote(lax.rem(me + step, count)).start()
        return carry

    lax.fori_loop(1, count, send, 0)

    def drain(step, carry):
        peer = lax.rem(me + step, count)
        remote(peer).wait_send()
        pltpu.make_async_remote_copy(
            src_ref=x_ref.at[peer],
            dst_ref=o_ref.at[peer],
            send_sem=send_sem.at[peer],
            recv_sem=recv_sem.at[peer],
            device_id={"expert": peer},
            device_id_type=MESH,
        ).wait_recv()
        return carry

    lax.fori_loop(1, count, drain, 0)
    local.wait()


def all_to_all_kernel(x, collective_id):
    count = lax.axis_size("expert")
    shape = x.shape
    blocks = x.reshape(count, -1, shape[-1])
    out = pl.pallas_call(
        _all_to_all_kernel,
        out_shape=jax.ShapeDtypeStruct(blocks.shape, blocks.dtype),
        in_specs=[pl.BlockSpec(memory_space=pl.ANY)],
        out_specs=pl.BlockSpec(memory_space=pl.ANY),
        scratch_shapes=[
            pltpu.SemaphoreType.DMA((count,)),
            pltpu.SemaphoreType.DMA((count,)),
            pltpu.SemaphoreType.DMA(()),
        ],
        compiler_params=pltpu.CompilerParams(collective_id=collective_id, has_side_effects=True),
    )(blocks)
    return out.reshape(shape)


def _dp_gather_kernel(down_ref, up_ref, down_out, up_out, sems):
    me = lax.axis_index("dp")
    other = 1 - me
    barrier = pltpu.get_barrier_semaphore()
    pl.semaphore_signal(barrier, inc=1, device_id={"dp": other}, device_id_type=MESH)
    pl.semaphore_wait(barrier, 1)
    cols = down_ref.shape[1]
    rows = up_ref.shape[0]
    down_dst = down_out.at[:, pl.ds(pl.multiple_of(me * cols, cols), cols)]
    up_dst = up_out.at[pl.ds(pl.multiple_of(me * rows, rows), rows), :]
    copies = [
        pltpu.make_async_remote_copy(
            src_ref=down_ref,
            dst_ref=down_dst,
            send_sem=sems.at[0],
            recv_sem=sems.at[1],
            device_id={"dp": other},
            device_id_type=MESH,
        ),
        pltpu.make_async_remote_copy(
            src_ref=up_ref,
            dst_ref=up_dst,
            send_sem=sems.at[2],
            recv_sem=sems.at[3],
            device_id={"dp": other},
            device_id_type=MESH,
        ),
        pltpu.make_async_copy(down_ref, down_dst, sems.at[4]),
        pltpu.make_async_copy(up_ref, up_dst, sems.at[5]),
    ]
    for copy in copies:
        copy.start()
    for copy in copies:
        copy.wait()


def dp_gather(down, up):
    count = lax.axis_size("dp")
    return pl.pallas_call(
        _dp_gather_kernel,
        out_shape=(
            jax.ShapeDtypeStruct((down.shape[0], down.shape[1] * count), down.dtype),
            jax.ShapeDtypeStruct((up.shape[0] * count, up.shape[1]), up.dtype),
        ),
        in_specs=[pl.BlockSpec(memory_space=pltpu.VMEM)] * 2,
        out_specs=(pl.BlockSpec(memory_space=pl.ANY), pl.BlockSpec(memory_space=pl.ANY)),
        scratch_shapes=[pltpu.SemaphoreType.DMA((6,))],
        compiler_params=pltpu.CompilerParams(collective_id=5, has_side_effects=True),
    )(down, up)


def on_device(
    tokens,
    cotangent,
    expert_ids,
    slot_ids,
    gate_weights,
    latent_down,
    latent_up,
    expert_gate,
    expert_linear,
    expert_out,
):
    row_count = tokens.shape[0]
    pick_count = expert_ids.shape[1]
    local_count = expert_gate.shape[0]
    group_count = lax.axis_size("expert")
    expert_count = group_count * local_count
    capacity = min(
        row_count, 2 * ((9 * row_count * pick_count + 16 * expert_count - 1) // (16 * expert_count))
    )
    down_full, up_full = dp_gather(latent_down, latent_up)
    gate_full, linear_full, output_full = (
        lax.all_gather(expert_gate, "dp", axis=1, tiled=True),
        lax.all_gather(expert_linear, "dp", axis=1, tiled=True),
        lax.all_gather(expert_out, "dp", axis=2, tiled=True),
    )
    latent_part = jnp.dot(tokens, down_full, preferred_element_type=jnp.float32)
    back_part = lax.dot_general(
        cotangent, up_full, (((1,), (1,)), ((), ())), preferred_element_type=jnp.float32
    )
    width = latent_part.shape[1]
    both = pair_sum(jnp.concatenate([latent_part, back_part], axis=1), 1)
    latent = both[:, :width].astype(jnp.bfloat16)
    back_latent = both[:, width:]
    half_cap = capacity // 2
    side = lax.axis_index("half")
    swap = [(0, 1), (1, 0)]
    flat_slot = (expert_ids * capacity + slot_ids).reshape(-1)
    owned_shape = (expert_count, half_cap)
    owned_slot = (
        lax.broadcasted_iota(jnp.int32, owned_shape, 0) * capacity
        + side * half_cap
        + lax.broadcasted_iota(jnp.int32, owned_shape, 1)
    ).reshape(-1)
    matches = flat_slot[None, :] == owned_slot[:, None]
    choice_index = lax.broadcasted_iota(jnp.int32, matches.shape, 1)
    source = jnp.sum(jnp.where(matches, choice_index, 0), axis=1)
    filled = jnp.any(matches, axis=1)
    token_of = source // pick_count
    gate_of = gate_weights.reshape(-1)[source]
    send_latent = jnp.where(filled[:, None], latent[token_of], jnp.zeros((), jnp.bfloat16))
    send_back = jnp.where(filled[:, None], gate_of[:, None] * back_latent[token_of], 0.0).astype(
        jnp.bfloat16
    )
    send = jnp.concatenate([send_latent, send_back], axis=1)
    send = send.reshape(group_count, local_count, half_cap, 2 * width)
    mine = all_to_all_kernel(send, 3)
    theirs = lax.ppermute(mine, "half", swap)

    def forward(rows):
        rows_latent = rows[..., :width]
        rows_back = rows[..., width:]
        pre_gate = jnp.einsum(
            "neci,eih->nech", rows_latent, gate_full, preferred_element_type=jnp.float32
        )
        pre_linear = jnp.einsum(
            "neci,eih->nech", rows_latent, linear_full, preferred_element_type=jnp.float32
        )
        grad_hidden = jnp.einsum(
            "necj,ehj->nech", rows_back, output_full, preferred_element_type=jnp.float32
        )
        logistic = jax.nn.sigmoid(pre_gate)
        hidden = (pre_gate * logistic * pre_linear).astype(jnp.bfloat16)
        gate_delta = (
            grad_hidden * pre_linear * logistic * (1.0 + pre_gate * (1.0 - logistic))
        ).astype(jnp.bfloat16)
        linear_delta = (grad_hidden * pre_gate * logistic).astype(jnp.bfloat16)
        return rows_latent, rows_back, hidden, gate_delta, linear_delta

    def row_grad(gate_delta, linear_delta):
        row_part = jnp.einsum(
            "nech,eih->neci", gate_delta, gate_full, preferred_element_type=jnp.float32
        )
        return row_part + jnp.einsum(
            "nech,eih->neci", linear_delta, linear_full, preferred_element_type=jnp.float32
        )

    def weight_grads(rows_latent, rows_back, hidden, gate_delta, linear_delta):
        gate_part = jnp.einsum(
            "neci,nech->eih", rows_latent, gate_delta, preferred_element_type=jnp.float32
        )
        linear_part = jnp.einsum(
            "neci,nech->eih", rows_latent, linear_delta, preferred_element_type=jnp.float32
        )
        out_part = jnp.einsum(
            "nech,necj->ehj", hidden, rows_back, preferred_element_type=jnp.float32
        )
        return gate_part, linear_part, out_part

    own = forward(mine)
    own_row = row_grad(own[3], own[4])
    own_parts = weight_grads(*own)
    theirs, own_row, own_parts = lax.optimization_barrier((theirs, own_row, own_parts))
    other = forward(theirs)
    send_rows = row_grad(other[3], other[4]).astype(jnp.bfloat16)
    send_rows, other = lax.optimization_barrier((send_rows, other))
    other_rows = lax.ppermute(send_rows, "half", swap)
    other_parts = weight_grads(*other)
    other_rows, other_parts = lax.optimization_barrier((other_rows, other_parts))
    own_rows = own_row + other_rows.astype(jnp.float32)
    gate_part, linear_part, out_part = (a + b for a, b in zip(own_parts, other_parts))
    gate_share, linear_share, out_share = (
        lax.psum_scatter(
            gate_part.astype(jnp.bfloat16), "dp", scatter_dimension=1, tiled=True
        ).astype(jnp.float32),
        lax.psum_scatter(
            linear_part.astype(jnp.bfloat16), "dp", scatter_dimension=1, tiled=True
        ).astype(jnp.float32),
        lax.psum_scatter(
            out_part.astype(jnp.bfloat16), "dp", scatter_dimension=2, tiled=True
        ).astype(jnp.float32),
    )
    returned = all_to_all_kernel(own_rows.astype(jnp.bfloat16), 4)
    slot_rel = slot_ids - side * half_cap
    owned = (slot_rel >= 0) & (slot_rel < half_cap)
    position = expert_ids * half_cap + jnp.clip(slot_rel, 0, half_cap - 1)
    gathered = returned.reshape(expert_count * half_cap, width)[position]
    latent_half = jnp.sum(jnp.where(owned[..., None], gathered.astype(jnp.float32), 0.0), axis=1)
    latent_grad = pair_sum(latent_half, 2)
    token_grad = lax.dot_general(
        latent_grad.astype(jnp.bfloat16),
        down_full,
        (((1,), (1,)), ((), ())),
        preferred_element_type=jnp.float32,
    )
    return (
        token_grad.astype(jnp.bfloat16),
        gate_share.astype(jnp.bfloat16),
        linear_share.astype(jnp.bfloat16),
        out_share.astype(jnp.bfloat16),
    )


def solution(mesh):
    in_specs = (
        P(("expert", "dp"), "half"),
        P(("expert", "dp"), "half"),
        P(("expert", "dp"), None),
        P(("expert", "dp"), None),
        P(("expert", "dp"), None),
        P("half", "dp"),
        P("dp", "half"),
        P("expert", "dp", "half"),
        P("expert", "dp", "half"),
        P("expert", "half", "dp"),
    )
    out_specs = (
        P(("expert", "dp"), "half"),
        P("expert", "dp", "half"),
        P("expert", "dp", "half"),
        P("expert", "half", "dp"),
    )
    return jax.shard_map(
        on_device, mesh=mesh, in_specs=in_specs, out_specs=out_specs, check_vma=False
    )
```

```python
import functools

import jax
import jax.numpy as jnp
from jax import lax
from jax.experimental import pallas as pl
from jax.experimental.pallas import tpu as pltpu
from jax.sharding import PartitionSpec as P

MESH = pl.DeviceIdType.MESH


def _pair_sum_kernel(x_ref, o_ref, buf, send_sem, recv_sem):
    other = 1 - lax.axis_index("half")
    barrier = pltpu.get_barrier_semaphore()
    pl.semaphore_signal(barrier, inc=1, device_id={"half": other}, device_id_type=MESH)
    pl.semaphore_wait(barrier, 1)
    copy = pltpu.make_async_remote_copy(
        src_ref=x_ref,
        dst_ref=buf,
        send_sem=send_sem,
        recv_sem=recv_sem,
        device_id={"half": other},
        device_id_type=MESH,
    )
    copy.start()
    copy.wait()
    o_ref[...] = x_ref[...].astype(jnp.float32) + buf[...].astype(jnp.float32)


def pair_sum(x, collective_id):
    x = x.astype(jnp.bfloat16)
    return pl.pallas_call(
        _pair_sum_kernel,
        out_shape=jax.ShapeDtypeStruct(x.shape, jnp.float32),
        in_specs=[pl.BlockSpec(memory_space=pltpu.VMEM)],
        out_specs=pl.BlockSpec(memory_space=pltpu.VMEM),
        scratch_shapes=[
            pltpu.VMEM(x.shape, x.dtype),
            pltpu.SemaphoreType.DMA(()),
            pltpu.SemaphoreType.DMA(()),
        ],
        compiler_params=pltpu.CompilerParams(collective_id=collective_id, has_side_effects=True),
    )(x)


def _all_to_all_kernel(x_ref, o_ref, send_sem, recv_sem, local_sem):
    count = x_ref.shape[0]
    me = lax.axis_index("expert")
    barrier = pltpu.get_barrier_semaphore()

    def greet(step, carry):
        peer = lax.rem(me + step, count)
        pl.semaphore_signal(barrier, inc=1, device_id={"expert": peer}, device_id_type=MESH)
        return carry

    lax.fori_loop(1, count, greet, 0)
    pl.semaphore_wait(barrier, count - 1)
    local = pltpu.make_async_copy(x_ref.at[me], o_ref.at[me], local_sem)
    local.start()

    def remote(peer):
        return pltpu.make_async_remote_copy(
            src_ref=x_ref.at[peer],
            dst_ref=o_ref.at[me],
            send_sem=send_sem.at[peer],
            recv_sem=recv_sem.at[me],
            device_id={"expert": peer},
            device_id_type=MESH,
        )

    def send(step, carry):
        remote(lax.rem(me + step, count)).start()
        return carry

    lax.fori_loop(1, count, send, 0)

    def drain(step, carry):
        peer = lax.rem(me + step, count)
        remote(peer).wait_send()
        pltpu.make_async_remote_copy(
            src_ref=x_ref.at[peer],
            dst_ref=o_ref.at[peer],
            send_sem=send_sem.at[peer],
            recv_sem=recv_sem.at[peer],
            device_id={"expert": peer},
            device_id_type=MESH,
        ).wait_recv()
        return carry

    lax.fori_loop(1, count, drain, 0)
    local.wait()


def all_to_all_kernel(x, collective_id):
    count = lax.axis_size("expert")
    shape = x.shape
    blocks = x.reshape(count, -1, shape[-1])
    out = pl.pallas_call(
        _all_to_all_kernel,
        out_shape=jax.ShapeDtypeStruct(blocks.shape, blocks.dtype),
        in_specs=[pl.BlockSpec(memory_space=pl.ANY)],
        out_specs=pl.BlockSpec(memory_space=pl.ANY),
        scratch_shapes=[
            pltpu.SemaphoreType.DMA((count,)),
            pltpu.SemaphoreType.DMA((count,)),
            pltpu.SemaphoreType.DMA(()),
        ],
        compiler_params=pltpu.CompilerParams(collective_id=collective_id, has_side_effects=True),
    )(blocks)
    return out.reshape(shape)


def _dp_gather_kernel(down_ref, up_ref, down_out, up_out, sems):
    me = lax.axis_index("dp")
    other = 1 - me
    barrier = pltpu.get_barrier_semaphore()
    pl.semaphore_signal(barrier, inc=1, device_id={"dp": other}, device_id_type=MESH)
    pl.semaphore_wait(barrier, 1)
    cols = down_ref.shape[1]
    rows = up_ref.shape[0]
    down_dst = down_out.at[:, pl.ds(pl.multiple_of(me * cols, cols), cols)]
    up_dst = up_out.at[pl.ds(pl.multiple_of(me * rows, rows), rows), :]
    copies = [
        pltpu.make_async_remote_copy(
            src_ref=down_ref,
            dst_ref=down_dst,
            send_sem=sems.at[0],
            recv_sem=sems.at[1],
            device_id={"dp": other},
            device_id_type=MESH,
        ),
        pltpu.make_async_remote_copy(
            src_ref=up_ref,
            dst_ref=up_dst,
            send_sem=sems.at[2],
            recv_sem=sems.at[3],
            device_id={"dp": other},
            device_id_type=MESH,
        ),
        pltpu.make_async_copy(down_ref, down_dst, sems.at[4]),
        pltpu.make_async_copy(up_ref, up_dst, sems.at[5]),
    ]
    for copy in copies:
        copy.start()
    for copy in copies:
        copy.wait()


def dp_gather(down, up):
    count = lax.axis_size("dp")
    return pl.pallas_call(
        _dp_gather_kernel,
        out_shape=(
            jax.ShapeDtypeStruct((down.shape[0], down.shape[1] * count), down.dtype),
            jax.ShapeDtypeStruct((up.shape[0] * count, up.shape[1]), up.dtype),
        ),
        in_specs=[pl.BlockSpec(memory_space=pltpu.VMEM)] * 2,
        out_specs=(pl.BlockSpec(memory_space=pl.ANY), pl.BlockSpec(memory_space=pl.ANY)),
        scratch_shapes=[pltpu.SemaphoreType.DMA((6,))],
        compiler_params=pltpu.CompilerParams(collective_id=5, has_side_effects=True),
    )(down, up)


def on_device(
    tokens,
    cotangent,
    expert_ids,
    slot_ids,
    gate_weights,
    latent_down,
    latent_up,
    expert_gate,
    expert_linear,
    expert_out,
):
    row_count = tokens.shape[0]
    pick_count = expert_ids.shape[1]
    local_count = expert_gate.shape[0]
    group_count = lax.axis_size("expert")
    expert_count = group_count * local_count
    capacity = min(
        row_count, 2 * ((9 * row_count * pick_count + 16 * expert_count - 1) // (16 * expert_count))
    )
    down_full, up_full = dp_gather(latent_down, latent_up)
    gate_full, linear_full, output_full = (
        lax.all_gather(expert_gate, "dp", axis=1, tiled=True),
        lax.all_gather(expert_linear, "dp", axis=1, tiled=True),
        lax.all_gather(expert_out, "dp", axis=2, tiled=True),
    )
    latent_part = jnp.dot(tokens, down_full, preferred_element_type=jnp.float32)
    back_part = lax.dot_general(
        cotangent, up_full, (((1,), (1,)), ((), ())), preferred_element_type=jnp.float32
    )
    width = latent_part.shape[1]
    both = pair_sum(jnp.concatenate([latent_part, back_part], axis=1), 1)
    latent = both[:, :width].astype(jnp.bfloat16)
    back_latent = both[:, width:]
    half_cap = capacity // 2
    side = lax.axis_index("half")
    swap = [(0, 1), (1, 0)]
    flat_slot = (expert_ids * capacity + slot_ids).reshape(-1)
    owned_shape = (expert_count, half_cap)
    owned_slot = (
        lax.broadcasted_iota(jnp.int32, owned_shape, 0) * capacity
        + side * half_cap
        + lax.broadcasted_iota(jnp.int32, owned_shape, 1)
    ).reshape(-1)
    matches = (flat_slot[None, :] == owned_slot[:, None]).reshape(-1, row_count, pick_count)
    picks = jnp.any(matches, axis=2).astype(jnp.bfloat16)
    weights = jnp.sum(jnp.where(matches, gate_weights[None], 0.0), axis=2)
    send_latent = jnp.dot(picks, latent, preferred_element_type=jnp.float32).astype(jnp.bfloat16)
    send_back = jnp.dot(
        weights,
        back_latent,
        precision=lax.Precision.HIGHEST,
        preferred_element_type=jnp.float32,
    ).astype(jnp.bfloat16)
    send = jnp.concatenate([send_latent, send_back], axis=1)
    send = send.reshape(group_count, local_count, half_cap, 2 * width)
    mine = all_to_all_kernel(send, 3)
    theirs = lax.ppermute(mine, "half", swap)

    def forward(rows):
        rows_latent = rows[..., :width]
        rows_back = rows[..., width:]
        pre_gate = jnp.einsum(
            "neci,eih->nech", rows_latent, gate_full, preferred_element_type=jnp.float32
        )
        pre_linear = jnp.einsum(
            "neci,eih->nech", rows_latent, linear_full, preferred_element_type=jnp.float32
        )
        grad_hidden = jnp.einsum(
            "necj,ehj->nech", rows_back, output_full, preferred_element_type=jnp.float32
        )
        logistic = jax.nn.sigmoid(pre_gate)
        hidden = (pre_gate * logistic * pre_linear).astype(jnp.bfloat16)
        gate_delta = (
            grad_hidden * pre_linear * logistic * (1.0 + pre_gate * (1.0 - logistic))
        ).astype(jnp.bfloat16)
        linear_delta = (grad_hidden * pre_gate * logistic).astype(jnp.bfloat16)
        return rows_latent, rows_back, hidden, gate_delta, linear_delta

    def row_grad(gate_delta, linear_delta):
        row_part = jnp.einsum(
            "nech,eih->neci", gate_delta, gate_full, preferred_element_type=jnp.float32
        )
        return row_part + jnp.einsum(
            "nech,eih->neci", linear_delta, linear_full, preferred_element_type=jnp.float32
        )

    def weight_grads(rows_latent, rows_back, hidden, gate_delta, linear_delta):
        gate_part = jnp.einsum(
            "neci,nech->eih", rows_latent, gate_delta, preferred_element_type=jnp.float32
        )
        linear_part = jnp.einsum(
            "neci,nech->eih", rows_latent, linear_delta, preferred_element_type=jnp.float32
        )
        out_part = jnp.einsum(
            "nech,necj->ehj", hidden, rows_back, preferred_element_type=jnp.float32
        )
        return gate_part, linear_part, out_part

    own = forward(mine)
    own_row = row_grad(own[3], own[4])
    own_parts = weight_grads(*own)
    theirs, own_row, own_parts = lax.optimization_barrier((theirs, own_row, own_parts))
    other = forward(theirs)
    send_rows = row_grad(other[3], other[4]).astype(jnp.bfloat16)
    send_rows, other = lax.optimization_barrier((send_rows, other))
    other_rows = lax.ppermute(send_rows, "half", swap)
    other_parts = weight_grads(*other)
    other_rows, other_parts = lax.optimization_barrier((other_rows, other_parts))
    own_rows = own_row + other_rows.astype(jnp.float32)
    gate_part, linear_part, out_part = (a + b for a, b in zip(own_parts, other_parts))
    gate_share, linear_share, out_share = (
        lax.psum_scatter(
            gate_part.astype(jnp.bfloat16), "dp", scatter_dimension=1, tiled=True
        ).astype(jnp.float32),
        lax.psum_scatter(
            linear_part.astype(jnp.bfloat16), "dp", scatter_dimension=1, tiled=True
        ).astype(jnp.float32),
        lax.psum_scatter(
            out_part.astype(jnp.bfloat16), "dp", scatter_dimension=2, tiled=True
        ).astype(jnp.float32),
    )
    returned = all_to_all_kernel(own_rows.astype(jnp.bfloat16), 4)
    slot_rel = slot_ids - side * half_cap
    owned = (slot_rel >= 0) & (slot_rel < half_cap)
    position = jnp.where(owned, expert_ids * half_cap + slot_rel, -1).reshape(-1)
    slot_index = lax.broadcasted_iota(jnp.int32, (row_count * pick_count, expert_count * half_cap), 1)
    combine = (position[:, None] == slot_index).reshape(row_count, pick_count, -1)
    combine = jnp.any(combine, axis=1).astype(jnp.bfloat16)
    latent_half = jnp.dot(
        combine,
        returned.reshape(expert_count * half_cap, width),
        preferred_element_type=jnp.float32,
    )
    latent_grad = pair_sum(latent_half, 2)
    token_grad = lax.dot_general(
        latent_grad.astype(jnp.bfloat16),
        down_full,
        (((1,), (1,)), ((), ())),
        preferred_element_type=jnp.float32,
    )
    return (
        token_grad.astype(jnp.bfloat16),
        gate_share.astype(jnp.bfloat16),
        linear_share.astype(jnp.bfloat16),
        out_share.astype(jnp.bfloat16),
    )


def solution(mesh):
    in_specs = (
        P(("expert", "dp"), "half"),
        P(("expert", "dp"), "half"),
        P(("expert", "dp"), None),
        P(("expert", "dp"), None),
        P(("expert", "dp"), None),
        P("half", "dp"),
        P("dp", "half"),
        P("expert", "dp", "half"),
        P("expert", "dp", "half"),
        P("expert", "half", "dp"),
    )
    out_specs = (
        P(("expert", "dp"), "half"),
        P("expert", "dp", "half"),
        P("expert", "dp", "half"),
        P("expert", "half", "dp"),
    )
    return jax.shard_map(
        on_device, mesh=mesh, in_specs=in_specs, out_specs=out_specs, check_vma=False
    )
```

```python
import functools

import jax
import jax.numpy as jnp
from jax import lax
from jax.experimental import pallas as pl
from jax.experimental.pallas import tpu as pltpu
from jax.sharding import PartitionSpec as P

MESH = pl.DeviceIdType.MESH


def _pair_sum_kernel(x_ref, o_ref, buf, send_sem, recv_sem):
    other = 1 - lax.axis_index("half")
    barrier = pltpu.get_barrier_semaphore()
    pl.semaphore_signal(barrier, inc=1, device_id={"half": other}, device_id_type=MESH)
    pl.semaphore_wait(barrier, 1)
    copy = pltpu.make_async_remote_copy(
        src_ref=x_ref,
        dst_ref=buf,
        send_sem=send_sem,
        recv_sem=recv_sem,
        device_id={"half": other},
        device_id_type=MESH,
    )
    copy.start()
    copy.wait()
    o_ref[...] = x_ref[...].astype(jnp.float32) + buf[...].astype(jnp.float32)


def pair_sum(x, collective_id):
    x = x.astype(jnp.bfloat16)
    return pl.pallas_call(
        _pair_sum_kernel,
        out_shape=jax.ShapeDtypeStruct(x.shape, jnp.float32),
        in_specs=[pl.BlockSpec(memory_space=pltpu.VMEM)],
        out_specs=pl.BlockSpec(memory_space=pltpu.VMEM),
        scratch_shapes=[
            pltpu.VMEM(x.shape, x.dtype),
            pltpu.SemaphoreType.DMA(()),
            pltpu.SemaphoreType.DMA(()),
        ],
        compiler_params=pltpu.CompilerParams(collective_id=collective_id, has_side_effects=True),
    )(x)


def _all_to_all_kernel(x_ref, o_ref, send_sem, recv_sem, local_sem):
    count = x_ref.shape[0]
    me = lax.axis_index("expert")
    barrier = pltpu.get_barrier_semaphore()

    def greet(step, carry):
        peer = lax.rem(me + step, count)
        pl.semaphore_signal(barrier, inc=1, device_id={"expert": peer}, device_id_type=MESH)
        return carry

    lax.fori_loop(1, count, greet, 0)
    pl.semaphore_wait(barrier, count - 1)
    local = pltpu.make_async_copy(x_ref.at[me], o_ref.at[me], local_sem)
    local.start()

    def remote(peer):
        return pltpu.make_async_remote_copy(
            src_ref=x_ref.at[peer],
            dst_ref=o_ref.at[me],
            send_sem=send_sem.at[peer],
            recv_sem=recv_sem.at[me],
            device_id={"expert": peer},
            device_id_type=MESH,
        )

    def send(step, carry):
        remote(lax.rem(me + step, count)).start()
        return carry

    lax.fori_loop(1, count, send, 0)

    def drain(step, carry):
        peer = lax.rem(me + step, count)
        remote(peer).wait_send()
        pltpu.make_async_remote_copy(
            src_ref=x_ref.at[peer],
            dst_ref=o_ref.at[peer],
            send_sem=send_sem.at[peer],
            recv_sem=recv_sem.at[peer],
            device_id={"expert": peer},
            device_id_type=MESH,
        ).wait_recv()
        return carry

    lax.fori_loop(1, count, drain, 0)
    local.wait()


def all_to_all_kernel(x, collective_id):
    count = lax.axis_size("expert")
    shape = x.shape
    blocks = x.reshape(count, -1, shape[-1])
    out = pl.pallas_call(
        _all_to_all_kernel,
        out_shape=jax.ShapeDtypeStruct(blocks.shape, blocks.dtype),
        in_specs=[pl.BlockSpec(memory_space=pl.ANY)],
        out_specs=pl.BlockSpec(memory_space=pl.ANY),
        scratch_shapes=[
            pltpu.SemaphoreType.DMA((count,)),
            pltpu.SemaphoreType.DMA((count,)),
            pltpu.SemaphoreType.DMA(()),
        ],
        compiler_params=pltpu.CompilerParams(collective_id=collective_id, has_side_effects=True),
    )(blocks)
    return out.reshape(shape)


def _dp_gather_kernel(down_ref, up_ref, down_out, up_out, sems):
    me = lax.axis_index("dp")
    other = 1 - me
    barrier = pltpu.get_barrier_semaphore()
    pl.semaphore_signal(barrier, inc=1, device_id={"dp": other}, device_id_type=MESH)
    pl.semaphore_wait(barrier, 1)
    cols = down_ref.shape[1]
    rows = up_ref.shape[0]
    down_dst = down_out.at[:, pl.ds(pl.multiple_of(me * cols, cols), cols)]
    up_dst = up_out.at[pl.ds(pl.multiple_of(me * rows, rows), rows), :]
    copies = [
        pltpu.make_async_remote_copy(
            src_ref=down_ref,
            dst_ref=down_dst,
            send_sem=sems.at[0],
            recv_sem=sems.at[1],
            device_id={"dp": other},
            device_id_type=MESH,
        ),
        pltpu.make_async_remote_copy(
            src_ref=up_ref,
            dst_ref=up_dst,
            send_sem=sems.at[2],
            recv_sem=sems.at[3],
            device_id={"dp": other},
            device_id_type=MESH,
        ),
        pltpu.make_async_copy(down_ref, down_dst, sems.at[4]),
        pltpu.make_async_copy(up_ref, up_dst, sems.at[5]),
    ]
    for copy in copies:
        copy.start()
    for copy in copies:
        copy.wait()


def dp_gather(down, up):
    count = lax.axis_size("dp")
    return pl.pallas_call(
        _dp_gather_kernel,
        out_shape=(
            jax.ShapeDtypeStruct((down.shape[0], down.shape[1] * count), down.dtype),
            jax.ShapeDtypeStruct((up.shape[0] * count, up.shape[1]), up.dtype),
        ),
        in_specs=[pl.BlockSpec(memory_space=pltpu.VMEM)] * 2,
        out_specs=(pl.BlockSpec(memory_space=pl.ANY), pl.BlockSpec(memory_space=pl.ANY)),
        scratch_shapes=[pltpu.SemaphoreType.DMA((6,))],
        compiler_params=pltpu.CompilerParams(collective_id=5, has_side_effects=True),
    )(down, up)


def on_device(
    tokens,
    cotangent,
    expert_ids,
    slot_ids,
    gate_weights,
    latent_down,
    latent_up,
    expert_gate,
    expert_linear,
    expert_out,
):
    row_count = tokens.shape[0]
    pick_count = expert_ids.shape[1]
    local_count = expert_gate.shape[0]
    group_count = lax.axis_size("expert")
    expert_count = group_count * local_count
    capacity = min(
        row_count, 2 * ((9 * row_count * pick_count + 16 * expert_count - 1) // (16 * expert_count))
    )
    down_full, up_full = dp_gather(latent_down, latent_up)
    gate_full, linear_full, output_full = (
        lax.all_gather(expert_gate, "dp", axis=1, tiled=True),
        lax.all_gather(expert_linear, "dp", axis=1, tiled=True),
        lax.all_gather(expert_out, "dp", axis=2, tiled=True),
    )
    latent_part = jnp.dot(tokens, down_full, preferred_element_type=jnp.float32)
    back_part = lax.dot_general(
        cotangent, up_full, (((1,), (1,)), ((), ())), preferred_element_type=jnp.float32
    )
    width = latent_part.shape[1]
    both = pair_sum(jnp.concatenate([latent_part, back_part], axis=1), 1)
    latent = both[:, :width].astype(jnp.bfloat16)
    back_latent = both[:, width:]
    half_cap = capacity // 2
    side = lax.axis_index("half")
    swap = [(0, 1), (1, 0)]
    flat_slot = (expert_ids * capacity + slot_ids).reshape(-1)
    owned_shape = (expert_count, half_cap)
    owned_slot = (
        lax.broadcasted_iota(jnp.int32, owned_shape, 0) * capacity
        + side * half_cap
        + lax.broadcasted_iota(jnp.int32, owned_shape, 1)
    ).reshape(-1)
    matches = (flat_slot[None, :] == owned_slot[:, None]).reshape(-1, row_count, pick_count)
    picks = jnp.any(matches, axis=2).astype(jnp.bfloat16)
    weights = jnp.sum(jnp.where(matches, gate_weights[None], 0.0), axis=2)
    send_latent = jnp.dot(picks, latent, preferred_element_type=jnp.float32).astype(jnp.bfloat16)
    send_back = jnp.dot(
        weights,
        back_latent,
        precision=lax.Precision.HIGHEST,
        preferred_element_type=jnp.float32,
    ).astype(jnp.bfloat16)
    block_shape = (group_count, local_count, half_cap, width)
    mine_latent = all_to_all_kernel(send_latent.reshape(block_shape), 3)
    theirs_latent = lax.ppermute(mine_latent, "half", swap)
    mine_back = all_to_all_kernel(send_back.reshape(block_shape), 6)
    theirs_back = lax.ppermute(mine_back, "half", swap)
    mine = (mine_latent, mine_back)
    theirs = (theirs_latent, theirs_back)

    def forward(rows):
        rows_latent, rows_back = rows
        pre_gate = jnp.einsum(
            "neci,eih->nech", rows_latent, gate_full, preferred_element_type=jnp.float32
        )
        pre_linear = jnp.einsum(
            "neci,eih->nech", rows_latent, linear_full, preferred_element_type=jnp.float32
        )
        grad_hidden = jnp.einsum(
            "necj,ehj->nech", rows_back, output_full, preferred_element_type=jnp.float32
        )
        logistic = jax.nn.sigmoid(pre_gate)
        hidden = (pre_gate * logistic * pre_linear).astype(jnp.bfloat16)
        gate_delta = (
            grad_hidden * pre_linear * logistic * (1.0 + pre_gate * (1.0 - logistic))
        ).astype(jnp.bfloat16)
        linear_delta = (grad_hidden * pre_gate * logistic).astype(jnp.bfloat16)
        return rows_latent, rows_back, hidden, gate_delta, linear_delta

    def row_grad(gate_delta, linear_delta):
        row_part = jnp.einsum(
            "nech,eih->neci", gate_delta, gate_full, preferred_element_type=jnp.float32
        )
        return row_part + jnp.einsum(
            "nech,eih->neci", linear_delta, linear_full, preferred_element_type=jnp.float32
        )

    def weight_grads(rows_latent, rows_back, hidden, gate_delta, linear_delta):
        gate_part = jnp.einsum(
            "neci,nech->eih", rows_latent, gate_delta, preferred_element_type=jnp.float32
        )
        linear_part = jnp.einsum(
            "neci,nech->eih", rows_latent, linear_delta, preferred_element_type=jnp.float32
        )
        out_part = jnp.einsum(
            "nech,necj->ehj", hidden, rows_back, preferred_element_type=jnp.float32
        )
        return gate_part, linear_part, out_part

    own = forward(mine)
    own_row = row_grad(own[3], own[4])
    own_parts = weight_grads(*own)
    theirs, own_row, own_parts = lax.optimization_barrier((theirs, own_row, own_parts))
    other = forward(theirs)
    send_rows = row_grad(other[3], other[4]).astype(jnp.bfloat16)
    send_rows, other = lax.optimization_barrier((send_rows, other))
    other_rows = lax.ppermute(send_rows, "half", swap)
    other_parts = weight_grads(*other)
    other_rows, other_parts = lax.optimization_barrier((other_rows, other_parts))
    own_rows = own_row + other_rows.astype(jnp.float32)
    gate_part, linear_part, out_part = (a + b for a, b in zip(own_parts, other_parts))
    gate_share, linear_share, out_share = (
        lax.psum_scatter(
            gate_part.astype(jnp.bfloat16), "dp", scatter_dimension=1, tiled=True
        ).astype(jnp.float32),
        lax.psum_scatter(
            linear_part.astype(jnp.bfloat16), "dp", scatter_dimension=1, tiled=True
        ).astype(jnp.float32),
        lax.psum_scatter(
            out_part.astype(jnp.bfloat16), "dp", scatter_dimension=2, tiled=True
        ).astype(jnp.float32),
    )
    returned = all_to_all_kernel(own_rows.astype(jnp.bfloat16), 4)
    slot_rel = slot_ids - side * half_cap
    owned = (slot_rel >= 0) & (slot_rel < half_cap)
    position = jnp.where(owned, expert_ids * half_cap + slot_rel, -1).reshape(-1)
    slot_index = lax.broadcasted_iota(jnp.int32, (row_count * pick_count, expert_count * half_cap), 1)
    combine = (position[:, None] == slot_index).reshape(row_count, pick_count, -1)
    combine = jnp.any(combine, axis=1).astype(jnp.bfloat16)
    latent_half = jnp.dot(
        combine,
        returned.reshape(expert_count * half_cap, width),
        preferred_element_type=jnp.float32,
    )
    latent_grad = pair_sum(latent_half, 2)
    token_grad = lax.dot_general(
        latent_grad.astype(jnp.bfloat16),
        down_full,
        (((1,), (1,)), ((), ())),
        preferred_element_type=jnp.float32,
    )
    return (
        token_grad.astype(jnp.bfloat16),
        gate_share.astype(jnp.bfloat16),
        linear_share.astype(jnp.bfloat16),
        out_share.astype(jnp.bfloat16),
    )


def solution(mesh):
    in_specs = (
        P(("expert", "dp"), "half"),
        P(("expert", "dp"), "half"),
        P(("expert", "dp"), None),
        P(("expert", "dp"), None),
        P(("expert", "dp"), None),
        P("half", "dp"),
        P("dp", "half"),
        P("expert", "dp", "half"),
        P("expert", "dp", "half"),
        P("expert", "half", "dp"),
    )
    out_specs = (
        P(("expert", "dp"), "half"),
        P("expert", "dp", "half"),
        P("expert", "dp", "half"),
        P("expert", "half", "dp"),
    )
    return jax.shard_map(
        on_device, mesh=mesh, in_specs=in_specs, out_specs=out_specs, check_vma=False
    )
```

```python
import functools

import jax
import jax.numpy as jnp
from jax import lax
from jax.experimental import pallas as pl
from jax.experimental.pallas import tpu as pltpu
from jax.sharding import PartitionSpec as P

MESH = pl.DeviceIdType.MESH


def _pair_sum_kernel(x_ref, o_ref, buf, send_sem, recv_sem):
    other = 1 - lax.axis_index("half")
    barrier = pltpu.get_barrier_semaphore()
    pl.semaphore_signal(barrier, inc=1, device_id={"half": other}, device_id_type=MESH)
    pl.semaphore_wait(barrier, 1)
    copy = pltpu.make_async_remote_copy(
        src_ref=x_ref,
        dst_ref=buf,
        send_sem=send_sem,
        recv_sem=recv_sem,
        device_id={"half": other},
        device_id_type=MESH,
    )
    copy.start()
    copy.wait()
    o_ref[...] = x_ref[...].astype(jnp.float32) + buf[...].astype(jnp.float32)


def pair_sum(x, collective_id):
    x = x.astype(jnp.bfloat16)
    return pl.pallas_call(
        _pair_sum_kernel,
        out_shape=jax.ShapeDtypeStruct(x.shape, jnp.float32),
        in_specs=[pl.BlockSpec(memory_space=pltpu.VMEM)],
        out_specs=pl.BlockSpec(memory_space=pltpu.VMEM),
        scratch_shapes=[
            pltpu.VMEM(x.shape, x.dtype),
            pltpu.SemaphoreType.DMA(()),
            pltpu.SemaphoreType.DMA(()),
        ],
        compiler_params=pltpu.CompilerParams(collective_id=collective_id, has_side_effects=True),
    )(x)


def _all_to_all_kernel(x_ref, o_ref, send_sem, recv_sem, local_sem):
    count = x_ref.shape[0]
    me = lax.axis_index("expert")
    barrier = pltpu.get_barrier_semaphore()

    def greet(step, carry):
        peer = lax.rem(me + step, count)
        pl.semaphore_signal(barrier, inc=1, device_id={"expert": peer}, device_id_type=MESH)
        return carry

    lax.fori_loop(1, count, greet, 0)
    pl.semaphore_wait(barrier, count - 1)
    local = pltpu.make_async_copy(x_ref.at[me], o_ref.at[me], local_sem)
    local.start()

    def remote(peer):
        return pltpu.make_async_remote_copy(
            src_ref=x_ref.at[peer],
            dst_ref=o_ref.at[me],
            send_sem=send_sem.at[peer],
            recv_sem=recv_sem.at[me],
            device_id={"expert": peer},
            device_id_type=MESH,
        )

    def send(step, carry):
        remote(lax.rem(me + step, count)).start()
        return carry

    lax.fori_loop(1, count, send, 0)

    def drain(step, carry):
        peer = lax.rem(me + step, count)
        remote(peer).wait_send()
        pltpu.make_async_remote_copy(
            src_ref=x_ref.at[peer],
            dst_ref=o_ref.at[peer],
            send_sem=send_sem.at[peer],
            recv_sem=recv_sem.at[peer],
            device_id={"expert": peer},
            device_id_type=MESH,
        ).wait_recv()
        return carry

    lax.fori_loop(1, count, drain, 0)
    local.wait()


def all_to_all_kernel(x, collective_id):
    count = lax.axis_size("expert")
    shape = x.shape
    blocks = x.reshape(count, -1, shape[-1])
    out = pl.pallas_call(
        _all_to_all_kernel,
        out_shape=jax.ShapeDtypeStruct(blocks.shape, blocks.dtype),
        in_specs=[pl.BlockSpec(memory_space=pl.ANY)],
        out_specs=pl.BlockSpec(memory_space=pl.ANY),
        scratch_shapes=[
            pltpu.SemaphoreType.DMA((count,)),
            pltpu.SemaphoreType.DMA((count,)),
            pltpu.SemaphoreType.DMA(()),
        ],
        compiler_params=pltpu.CompilerParams(collective_id=collective_id, has_side_effects=True),
    )(blocks)
    return out.reshape(shape)


def _dp_gather_kernel(down_ref, up_ref, down_out, up_out, sems):
    me = lax.axis_index("dp")
    other = 1 - me
    barrier = pltpu.get_barrier_semaphore()
    pl.semaphore_signal(barrier, inc=1, device_id={"dp": other}, device_id_type=MESH)
    pl.semaphore_wait(barrier, 1)
    cols = down_ref.shape[1]
    rows = up_ref.shape[0]
    down_dst = down_out.at[:, pl.ds(pl.multiple_of(me * cols, cols), cols)]
    up_dst = up_out.at[pl.ds(pl.multiple_of(me * rows, rows), rows), :]
    copies = [
        pltpu.make_async_remote_copy(
            src_ref=down_ref,
            dst_ref=down_dst,
            send_sem=sems.at[0],
            recv_sem=sems.at[1],
            device_id={"dp": other},
            device_id_type=MESH,
        ),
        pltpu.make_async_remote_copy(
            src_ref=up_ref,
            dst_ref=up_dst,
            send_sem=sems.at[2],
            recv_sem=sems.at[3],
            device_id={"dp": other},
            device_id_type=MESH,
        ),
        pltpu.make_async_copy(down_ref, down_dst, sems.at[4]),
        pltpu.make_async_copy(up_ref, up_dst, sems.at[5]),
    ]
    for copy in copies:
        copy.start()
    for copy in copies:
        copy.wait()


def dp_gather(down, up):
    count = lax.axis_size("dp")
    return pl.pallas_call(
        _dp_gather_kernel,
        out_shape=(
            jax.ShapeDtypeStruct((down.shape[0], down.shape[1] * count), down.dtype),
            jax.ShapeDtypeStruct((up.shape[0] * count, up.shape[1]), up.dtype),
        ),
        in_specs=[pl.BlockSpec(memory_space=pltpu.VMEM)] * 2,
        out_specs=(pl.BlockSpec(memory_space=pl.ANY), pl.BlockSpec(memory_space=pl.ANY)),
        scratch_shapes=[pltpu.SemaphoreType.DMA((6,))],
        compiler_params=pltpu.CompilerParams(collective_id=5, has_side_effects=True),
    )(down, up)


def on_device(
    tokens,
    cotangent,
    expert_ids,
    slot_ids,
    gate_weights,
    latent_down,
    latent_up,
    expert_gate,
    expert_linear,
    expert_out,
):
    row_count = tokens.shape[0]
    pick_count = expert_ids.shape[1]
    local_count = expert_gate.shape[0]
    group_count = lax.axis_size("expert")
    expert_count = group_count * local_count
    capacity = min(
        row_count, 2 * ((9 * row_count * pick_count + 16 * expert_count - 1) // (16 * expert_count))
    )
    down_full, up_full = dp_gather(latent_down, latent_up)
    gate_full, linear_full, output_full = (
        lax.all_gather(expert_gate, "dp", axis=1, tiled=True),
        lax.all_gather(expert_linear, "dp", axis=1, tiled=True),
        lax.all_gather(expert_out, "dp", axis=2, tiled=True),
    )
    latent_part = jnp.dot(tokens, down_full, preferred_element_type=jnp.float32)
    back_part = lax.dot_general(
        cotangent, up_full, (((1,), (1,)), ((), ())), preferred_element_type=jnp.float32
    )
    width = latent_part.shape[1]
    both = pair_sum(jnp.concatenate([latent_part, back_part], axis=1), 1)
    latent = both[:, :width].astype(jnp.bfloat16)
    back_latent = both[:, width:]
    half_cap = capacity // 2
    side = lax.axis_index("half")
    swap = [(0, 1), (1, 0)]
    flat_slot = (expert_ids * capacity + slot_ids).reshape(-1)
    owned_shape = (expert_count, half_cap)
    owned_slot = (
        lax.broadcasted_iota(jnp.int32, owned_shape, 0) * capacity
        + side * half_cap
        + lax.broadcasted_iota(jnp.int32, owned_shape, 1)
    ).reshape(-1)
    matches = (flat_slot[None, :] == owned_slot[:, None]).reshape(-1, row_count, pick_count)
    picks = jnp.any(matches, axis=2).astype(jnp.bfloat16)
    weights = jnp.sum(jnp.where(matches, gate_weights[None], 0.0), axis=2)
    send_latent = jnp.dot(picks, latent, preferred_element_type=jnp.float32).astype(jnp.bfloat16)
    send_back = jnp.dot(
        weights,
        back_latent,
        precision=lax.Precision.HIGHEST,
        preferred_element_type=jnp.float32,
    ).astype(jnp.bfloat16)
    block_shape = (group_count, local_count, half_cap, width)
    mine_latent = all_to_all_kernel(send_latent.reshape(block_shape), 3)
    theirs_latent = lax.ppermute(mine_latent, "half", swap)
    mine_back = all_to_all_kernel(send_back.reshape(block_shape), 6)
    theirs_back = lax.ppermute(mine_back, "half", swap)
    mine = (mine_latent, mine_back)
    theirs = (theirs_latent, theirs_back)

    def forward(rows):
        rows_latent, rows_back = rows
        pre_gate = jnp.einsum(
            "neci,eih->nech", rows_latent, gate_full, preferred_element_type=jnp.float32
        )
        pre_linear = jnp.einsum(
            "neci,eih->nech", rows_latent, linear_full, preferred_element_type=jnp.float32
        )
        grad_hidden = jnp.einsum(
            "necj,ehj->nech", rows_back, output_full, preferred_element_type=jnp.float32
        )
        logistic = jax.nn.sigmoid(pre_gate)
        hidden = (pre_gate * logistic * pre_linear).astype(jnp.bfloat16)
        gate_delta = (
            grad_hidden * pre_linear * logistic * (1.0 + pre_gate * (1.0 - logistic))
        ).astype(jnp.bfloat16)
        linear_delta = (grad_hidden * pre_gate * logistic).astype(jnp.bfloat16)
        return rows_latent, rows_back, hidden, gate_delta, linear_delta

    def row_grad(gate_delta, linear_delta):
        row_part = jnp.einsum(
            "nech,eih->neci", gate_delta, gate_full, preferred_element_type=jnp.float32
        )
        return row_part + jnp.einsum(
            "nech,eih->neci", linear_delta, linear_full, preferred_element_type=jnp.float32
        )

    def weight_grads(rows_latent, rows_back, hidden, gate_delta, linear_delta):
        gate_part = jnp.einsum(
            "neci,nech->eih", rows_latent, gate_delta, preferred_element_type=jnp.float32
        )
        linear_part = jnp.einsum(
            "neci,nech->eih", rows_latent, linear_delta, preferred_element_type=jnp.float32
        )
        out_part = jnp.einsum(
            "nech,necj->ehj", hidden, rows_back, preferred_element_type=jnp.float32
        )
        return gate_part, linear_part, out_part

    rows = tuple(jnp.concatenate(pair, axis=2) for pair in zip(mine, theirs))
    computed = forward(rows)
    row_all = row_grad(computed[3], computed[4])
    send_rows = row_all[:, :, half_cap:].astype(jnp.bfloat16)
    send_rows, computed = lax.optimization_barrier((send_rows, computed))
    other_rows = lax.ppermute(send_rows, "half", swap)
    parts = weight_grads(*computed)
    other_rows, parts = lax.optimization_barrier((other_rows, parts))
    own_rows = row_all[:, :, :half_cap] + other_rows.astype(jnp.float32)
    gate_part, linear_part, out_part = parts
    gate_share, linear_share, out_share = (
        lax.psum_scatter(
            gate_part.astype(jnp.bfloat16), "dp", scatter_dimension=1, tiled=True
        ).astype(jnp.float32),
        lax.psum_scatter(
            linear_part.astype(jnp.bfloat16), "dp", scatter_dimension=1, tiled=True
        ).astype(jnp.float32),
        lax.psum_scatter(
            out_part.astype(jnp.bfloat16), "dp", scatter_dimension=2, tiled=True
        ).astype(jnp.float32),
    )
    returned = all_to_all_kernel(own_rows.astype(jnp.bfloat16), 4)
    slot_rel = slot_ids - side * half_cap
    owned = (slot_rel >= 0) & (slot_rel < half_cap)
    position = jnp.where(owned, expert_ids * half_cap + slot_rel, -1).reshape(-1)
    slot_index = lax.broadcasted_iota(jnp.int32, (row_count * pick_count, expert_count * half_cap), 1)
    combine = (position[:, None] == slot_index).reshape(row_count, pick_count, -1)
    combine = jnp.any(combine, axis=1).astype(jnp.bfloat16)
    latent_half = jnp.dot(
        combine,
        returned.reshape(expert_count * half_cap, width),
        preferred_element_type=jnp.float32,
    )
    latent_grad = pair_sum(latent_half, 2)
    token_grad = lax.dot_general(
        latent_grad.astype(jnp.bfloat16),
        down_full,
        (((1,), (1,)), ((), ())),
        preferred_element_type=jnp.float32,
    )
    return (
        token_grad.astype(jnp.bfloat16),
        gate_share.astype(jnp.bfloat16),
        linear_share.astype(jnp.bfloat16),
        out_share.astype(jnp.bfloat16),
    )


def solution(mesh):
    in_specs = (
        P(("expert", "dp"), "half"),
        P(("expert", "dp"), "half"),
        P(("expert", "dp"), None),
        P(("expert", "dp"), None),
        P(("expert", "dp"), None),
        P("half", "dp"),
        P("dp", "half"),
        P("expert", "dp", "half"),
        P("expert", "dp", "half"),
        P("expert", "half", "dp"),
    )
    out_specs = (
        P(("expert", "dp"), "half"),
        P("expert", "dp", "half"),
        P("expert", "dp", "half"),
        P("expert", "half", "dp"),
    )
    return jax.shard_map(
        on_device, mesh=mesh, in_specs=in_specs, out_specs=out_specs, check_vma=False
    )
```

```python
import functools

import jax
import jax.numpy as jnp
from jax import lax
from jax.experimental import pallas as pl
from jax.experimental.pallas import tpu as pltpu
from jax.sharding import PartitionSpec as P

MESH = pl.DeviceIdType.MESH


def _pair_sum_kernel(x_ref, o_ref, buf, send_sem, recv_sem):
    other = 1 - lax.axis_index("half")
    barrier = pltpu.get_barrier_semaphore()
    pl.semaphore_signal(barrier, inc=1, device_id={"half": other}, device_id_type=MESH)
    pl.semaphore_wait(barrier, 1)
    copy = pltpu.make_async_remote_copy(
        src_ref=x_ref,
        dst_ref=buf,
        send_sem=send_sem,
        recv_sem=recv_sem,
        device_id={"half": other},
        device_id_type=MESH,
    )
    copy.start()
    copy.wait()
    o_ref[...] = x_ref[...].astype(jnp.float32) + buf[...].astype(jnp.float32)


def pair_sum(x, collective_id):
    x = x.astype(jnp.bfloat16)
    return pl.pallas_call(
        _pair_sum_kernel,
        out_shape=jax.ShapeDtypeStruct(x.shape, jnp.float32),
        in_specs=[pl.BlockSpec(memory_space=pltpu.VMEM)],
        out_specs=pl.BlockSpec(memory_space=pltpu.VMEM),
        scratch_shapes=[
            pltpu.VMEM(x.shape, x.dtype),
            pltpu.SemaphoreType.DMA(()),
            pltpu.SemaphoreType.DMA(()),
        ],
        compiler_params=pltpu.CompilerParams(collective_id=collective_id, has_side_effects=True),
    )(x)


def _all_to_all_kernel(x_ref, o_ref, send_sem, recv_sem, local_sem):
    count = x_ref.shape[0]
    me = lax.axis_index("expert")
    barrier = pltpu.get_barrier_semaphore()

    def greet(step, carry):
        peer = lax.rem(me + step, count)
        pl.semaphore_signal(barrier, inc=1, device_id={"expert": peer}, device_id_type=MESH)
        return carry

    lax.fori_loop(1, count, greet, 0)
    pl.semaphore_wait(barrier, count - 1)
    local = pltpu.make_async_copy(x_ref.at[me], o_ref.at[me], local_sem)
    local.start()

    def remote(peer):
        return pltpu.make_async_remote_copy(
            src_ref=x_ref.at[peer],
            dst_ref=o_ref.at[me],
            send_sem=send_sem.at[peer],
            recv_sem=recv_sem.at[me],
            device_id={"expert": peer},
            device_id_type=MESH,
        )

    def send(step, carry):
        remote(lax.rem(me + step, count)).start()
        return carry

    lax.fori_loop(1, count, send, 0)

    def drain(step, carry):
        peer = lax.rem(me + step, count)
        remote(peer).wait_send()
        pltpu.make_async_remote_copy(
            src_ref=x_ref.at[peer],
            dst_ref=o_ref.at[peer],
            send_sem=send_sem.at[peer],
            recv_sem=recv_sem.at[peer],
            device_id={"expert": peer},
            device_id_type=MESH,
        ).wait_recv()
        return carry

    lax.fori_loop(1, count, drain, 0)
    local.wait()


def all_to_all_kernel(x, collective_id):
    count = lax.axis_size("expert")
    shape = x.shape
    blocks = x.reshape(count, -1, shape[-1])
    out = pl.pallas_call(
        _all_to_all_kernel,
        out_shape=jax.ShapeDtypeStruct(blocks.shape, blocks.dtype),
        in_specs=[pl.BlockSpec(memory_space=pl.ANY)],
        out_specs=pl.BlockSpec(memory_space=pl.ANY),
        scratch_shapes=[
            pltpu.SemaphoreType.DMA((count,)),
            pltpu.SemaphoreType.DMA((count,)),
            pltpu.SemaphoreType.DMA(()),
        ],
        compiler_params=pltpu.CompilerParams(collective_id=collective_id, has_side_effects=True),
    )(blocks)
    return out.reshape(shape)


def _dp_gather_kernel(down_ref, up_ref, down_out, up_out, sems):
    me = lax.axis_index("dp")
    other = 1 - me
    barrier = pltpu.get_barrier_semaphore()
    pl.semaphore_signal(barrier, inc=1, device_id={"dp": other}, device_id_type=MESH)
    pl.semaphore_wait(barrier, 1)
    cols = down_ref.shape[1]
    rows = up_ref.shape[0]
    down_dst = down_out.at[:, pl.ds(pl.multiple_of(me * cols, cols), cols)]
    up_dst = up_out.at[pl.ds(pl.multiple_of(me * rows, rows), rows), :]
    copies = [
        pltpu.make_async_remote_copy(
            src_ref=down_ref,
            dst_ref=down_dst,
            send_sem=sems.at[0],
            recv_sem=sems.at[1],
            device_id={"dp": other},
            device_id_type=MESH,
        ),
        pltpu.make_async_remote_copy(
            src_ref=up_ref,
            dst_ref=up_dst,
            send_sem=sems.at[2],
            recv_sem=sems.at[3],
            device_id={"dp": other},
            device_id_type=MESH,
        ),
        pltpu.make_async_copy(down_ref, down_dst, sems.at[4]),
        pltpu.make_async_copy(up_ref, up_dst, sems.at[5]),
    ]
    for copy in copies:
        copy.start()
    for copy in copies:
        copy.wait()


def dp_gather(down, up):
    count = lax.axis_size("dp")
    return pl.pallas_call(
        _dp_gather_kernel,
        out_shape=(
            jax.ShapeDtypeStruct((down.shape[0], down.shape[1] * count), down.dtype),
            jax.ShapeDtypeStruct((up.shape[0] * count, up.shape[1]), up.dtype),
        ),
        in_specs=[pl.BlockSpec(memory_space=pltpu.VMEM)] * 2,
        out_specs=(pl.BlockSpec(memory_space=pl.ANY), pl.BlockSpec(memory_space=pl.ANY)),
        scratch_shapes=[pltpu.SemaphoreType.DMA((6,))],
        compiler_params=pltpu.CompilerParams(collective_id=5, has_side_effects=True),
    )(down, up)


def on_device(
    tokens,
    cotangent,
    expert_ids,
    slot_ids,
    gate_weights,
    latent_down,
    latent_up,
    expert_gate,
    expert_linear,
    expert_out,
):
    row_count = tokens.shape[0]
    pick_count = expert_ids.shape[1]
    local_count = expert_gate.shape[0]
    group_count = lax.axis_size("expert")
    expert_count = group_count * local_count
    capacity = min(
        row_count, 2 * ((9 * row_count * pick_count + 16 * expert_count - 1) // (16 * expert_count))
    )
    down_full, up_full = dp_gather(latent_down, latent_up)
    gate_full, linear_full, output_full = (
        lax.all_gather(expert_gate, "dp", axis=1, tiled=True),
        lax.all_gather(expert_linear, "dp", axis=1, tiled=True),
        lax.all_gather(expert_out, "dp", axis=2, tiled=True),
    )
    latent_part = jnp.dot(tokens, down_full, preferred_element_type=jnp.float32)
    back_part = lax.dot_general(
        cotangent, up_full, (((1,), (1,)), ((), ())), preferred_element_type=jnp.float32
    )
    width = latent_part.shape[1]
    both = pair_sum(jnp.concatenate([latent_part, back_part], axis=1), 1)
    latent = both[:, :width].astype(jnp.bfloat16)
    back_latent = both[:, width:]
    half_cap = capacity // 2
    side = lax.axis_index("half")
    swap = [(0, 1), (1, 0)]
    flat_slot = (expert_ids * capacity + slot_ids).reshape(-1)
    owned_shape = (expert_count, half_cap)
    owned_slot = (
        lax.broadcasted_iota(jnp.int32, owned_shape, 0) * capacity
        + side * half_cap
        + lax.broadcasted_iota(jnp.int32, owned_shape, 1)
    ).reshape(-1)
    matches = (flat_slot[None, :] == owned_slot[:, None]).reshape(-1, row_count, pick_count)
    picks = jnp.any(matches, axis=2).astype(jnp.bfloat16)
    weights = jnp.sum(jnp.where(matches, gate_weights[None], 0.0), axis=2)
    send_latent = jnp.dot(picks, latent, preferred_element_type=jnp.float32).astype(jnp.bfloat16)
    send_back = jnp.dot(
        weights,
        back_latent,
        precision=lax.Precision.HIGHEST,
        preferred_element_type=jnp.float32,
    ).astype(jnp.bfloat16)
    block_shape = (group_count, local_count, half_cap, width)
    mine_latent = all_to_all_kernel(send_latent.reshape(block_shape), 3)
    theirs_latent = lax.ppermute(mine_latent, "half", swap)
    mine_back = all_to_all_kernel(send_back.reshape(block_shape), 6)
    theirs_back = lax.ppermute(mine_back, "half", swap)
    mine = (mine_latent, mine_back)
    theirs = (theirs_latent, theirs_back)

    def forward(rows):
        rows_latent, rows_back = rows
        pre_gate = jnp.einsum(
            "neci,eih->nech", rows_latent, gate_full, preferred_element_type=jnp.float32
        )
        pre_linear = jnp.einsum(
            "neci,eih->nech", rows_latent, linear_full, preferred_element_type=jnp.float32
        )
        grad_hidden = jnp.einsum(
            "necj,ehj->nech", rows_back, output_full, preferred_element_type=jnp.float32
        )
        logistic = jax.nn.sigmoid(pre_gate)
        hidden = (pre_gate * logistic * pre_linear).astype(jnp.bfloat16)
        gate_delta = (
            grad_hidden * pre_linear * logistic * (1.0 + pre_gate * (1.0 - logistic))
        ).astype(jnp.bfloat16)
        linear_delta = (grad_hidden * pre_gate * logistic).astype(jnp.bfloat16)
        return rows_latent, rows_back, hidden, gate_delta, linear_delta

    def row_grad(gate_delta, linear_delta):
        row_part = jnp.einsum(
            "nech,eih->neci", gate_delta, gate_full, preferred_element_type=jnp.float32
        )
        return row_part + jnp.einsum(
            "nech,eih->neci", linear_delta, linear_full, preferred_element_type=jnp.float32
        )

    def weight_grads(rows_latent, rows_back, hidden, gate_delta, linear_delta):
        gate_part = jnp.einsum(
            "neci,nech->eih", rows_latent, gate_delta, preferred_element_type=jnp.float32
        )
        linear_part = jnp.einsum(
            "neci,nech->eih", rows_latent, linear_delta, preferred_element_type=jnp.float32
        )
        out_part = jnp.einsum(
            "nech,necj->ehj", hidden, rows_back, preferred_element_type=jnp.float32
        )
        return gate_part, linear_part, out_part

    own = forward(mine)
    own_row = row_grad(own[3], own[4])
    own_parts = weight_grads(*own)
    theirs, own_row, own_parts = lax.optimization_barrier((theirs, own_row, own_parts))
    other = forward(theirs)
    send_rows = row_grad(other[3], other[4]).astype(jnp.bfloat16)
    send_rows, other = lax.optimization_barrier((send_rows, other))
    other_rows = lax.ppermute(send_rows, "half", swap)
    other_parts = weight_grads(*other)
    parts = tuple((a + b).astype(jnp.bfloat16) for a, b in zip(own_parts, other_parts))
    other_rows, parts = lax.optimization_barrier((other_rows, parts))
    own_rows = own_row + other_rows.astype(jnp.float32)
    gate_part, linear_part, out_part = parts
    gate_share, linear_share, out_share = (
        lax.psum_scatter(
            gate_part.astype(jnp.bfloat16), "dp", scatter_dimension=1, tiled=True
        ).astype(jnp.float32),
        lax.psum_scatter(
            linear_part.astype(jnp.bfloat16), "dp", scatter_dimension=1, tiled=True
        ).astype(jnp.float32),
        lax.psum_scatter(
            out_part.astype(jnp.bfloat16), "dp", scatter_dimension=2, tiled=True
        ).astype(jnp.float32),
    )
    returned = all_to_all_kernel(own_rows.astype(jnp.bfloat16), 4)
    slot_rel = slot_ids - side * half_cap
    owned = (slot_rel >= 0) & (slot_rel < half_cap)
    position = jnp.where(owned, expert_ids * half_cap + slot_rel, -1).reshape(-1)
    slot_index = lax.broadcasted_iota(jnp.int32, (row_count * pick_count, expert_count * half_cap), 1)
    combine = (position[:, None] == slot_index).reshape(row_count, pick_count, -1)
    combine = jnp.any(combine, axis=1).astype(jnp.bfloat16)
    latent_half = jnp.dot(
        combine,
        returned.reshape(expert_count * half_cap, width),
        preferred_element_type=jnp.float32,
    )
    latent_grad = pair_sum(latent_half, 2)
    token_grad = lax.dot_general(
        latent_grad.astype(jnp.bfloat16),
        down_full,
        (((1,), (1,)), ((), ())),
        preferred_element_type=jnp.float32,
    )
    return (
        token_grad.astype(jnp.bfloat16),
        gate_share.astype(jnp.bfloat16),
        linear_share.astype(jnp.bfloat16),
        out_share.astype(jnp.bfloat16),
    )


def solution(mesh):
    in_specs = (
        P(("expert", "dp"), "half"),
        P(("expert", "dp"), "half"),
        P(("expert", "dp"), None),
        P(("expert", "dp"), None),
        P(("expert", "dp"), None),
        P("half", "dp"),
        P("dp", "half"),
        P("expert", "dp", "half"),
        P("expert", "dp", "half"),
        P("expert", "half", "dp"),
    )
    out_specs = (
        P(("expert", "dp"), "half"),
        P("expert", "dp", "half"),
        P("expert", "dp", "half"),
        P("expert", "half", "dp"),
    )
    return jax.shard_map(
        on_device, mesh=mesh, in_specs=in_specs, out_specs=out_specs, check_vma=False
    )
```

```python
import functools

import jax
import jax.numpy as jnp
from jax import lax
from jax.experimental import pallas as pl
from jax.experimental.pallas import tpu as pltpu
from jax.sharding import PartitionSpec as P

MESH = pl.DeviceIdType.MESH


def _pair_sum_kernel(x_ref, o_ref, buf, send_sem, recv_sem):
    other = 1 - lax.axis_index("half")
    barrier = pltpu.get_barrier_semaphore()
    pl.semaphore_signal(barrier, inc=1, device_id={"half": other}, device_id_type=MESH)
    pl.semaphore_wait(barrier, 1)
    copy = pltpu.make_async_remote_copy(
        src_ref=x_ref,
        dst_ref=buf,
        send_sem=send_sem,
        recv_sem=recv_sem,
        device_id={"half": other},
        device_id_type=MESH,
    )
    copy.start()
    copy.wait()
    o_ref[...] = x_ref[...].astype(jnp.float32) + buf[...].astype(jnp.float32)


def pair_sum(x, collective_id):
    x = x.astype(jnp.bfloat16)
    return pl.pallas_call(
        _pair_sum_kernel,
        out_shape=jax.ShapeDtypeStruct(x.shape, jnp.float32),
        in_specs=[pl.BlockSpec(memory_space=pltpu.VMEM)],
        out_specs=pl.BlockSpec(memory_space=pltpu.VMEM),
        scratch_shapes=[
            pltpu.VMEM(x.shape, x.dtype),
            pltpu.SemaphoreType.DMA(()),
            pltpu.SemaphoreType.DMA(()),
        ],
        compiler_params=pltpu.CompilerParams(collective_id=collective_id, has_side_effects=True),
    )(x)


def _all_to_all_kernel(x_ref, o_ref, send_sem, recv_sem, local_sem):
    count = x_ref.shape[0]
    me = lax.axis_index("expert")
    barrier = pltpu.get_barrier_semaphore()

    def greet(step, carry):
        peer = lax.rem(me + step, count)
        pl.semaphore_signal(barrier, inc=1, device_id={"expert": peer}, device_id_type=MESH)
        return carry

    lax.fori_loop(1, count, greet, 0)
    pl.semaphore_wait(barrier, count - 1)
    local = pltpu.make_async_copy(x_ref.at[me], o_ref.at[me], local_sem)
    local.start()

    def remote(peer):
        return pltpu.make_async_remote_copy(
            src_ref=x_ref.at[peer],
            dst_ref=o_ref.at[me],
            send_sem=send_sem.at[peer],
            recv_sem=recv_sem.at[me],
            device_id={"expert": peer},
            device_id_type=MESH,
        )

    def send(step, carry):
        remote(lax.rem(me + step, count)).start()
        return carry

    lax.fori_loop(1, count, send, 0)

    def drain(step, carry):
        peer = lax.rem(me + step, count)
        remote(peer).wait_send()
        pltpu.make_async_remote_copy(
            src_ref=x_ref.at[peer],
            dst_ref=o_ref.at[peer],
            send_sem=send_sem.at[peer],
            recv_sem=recv_sem.at[peer],
            device_id={"expert": peer},
            device_id_type=MESH,
        ).wait_recv()
        return carry

    lax.fori_loop(1, count, drain, 0)
    local.wait()


def all_to_all_kernel(x, collective_id):
    count = lax.axis_size("expert")
    shape = x.shape
    blocks = x.reshape(count, -1, shape[-1])
    out = pl.pallas_call(
        _all_to_all_kernel,
        out_shape=jax.ShapeDtypeStruct(blocks.shape, blocks.dtype),
        in_specs=[pl.BlockSpec(memory_space=pl.ANY)],
        out_specs=pl.BlockSpec(memory_space=pl.ANY),
        scratch_shapes=[
            pltpu.SemaphoreType.DMA((count,)),
            pltpu.SemaphoreType.DMA((count,)),
            pltpu.SemaphoreType.DMA(()),
        ],
        compiler_params=pltpu.CompilerParams(collective_id=collective_id, has_side_effects=True),
    )(blocks)
    return out.reshape(shape)


def _dp_gather_kernel(down_ref, up_ref, down_out, up_out, sems):
    me = lax.axis_index("dp")
    other = 1 - me
    barrier = pltpu.get_barrier_semaphore()
    pl.semaphore_signal(barrier, inc=1, device_id={"dp": other}, device_id_type=MESH)
    pl.semaphore_wait(barrier, 1)
    cols = down_ref.shape[1]
    rows = up_ref.shape[0]
    down_dst = down_out.at[:, pl.ds(pl.multiple_of(me * cols, cols), cols)]
    up_dst = up_out.at[pl.ds(pl.multiple_of(me * rows, rows), rows), :]
    copies = [
        pltpu.make_async_remote_copy(
            src_ref=down_ref,
            dst_ref=down_dst,
            send_sem=sems.at[0],
            recv_sem=sems.at[1],
            device_id={"dp": other},
            device_id_type=MESH,
        ),
        pltpu.make_async_remote_copy(
            src_ref=up_ref,
            dst_ref=up_dst,
            send_sem=sems.at[2],
            recv_sem=sems.at[3],
            device_id={"dp": other},
            device_id_type=MESH,
        ),
        pltpu.make_async_copy(down_ref, down_dst, sems.at[4]),
        pltpu.make_async_copy(up_ref, up_dst, sems.at[5]),
    ]
    for copy in copies:
        copy.start()
    for copy in copies:
        copy.wait()


def dp_gather(down, up):
    count = lax.axis_size("dp")
    return pl.pallas_call(
        _dp_gather_kernel,
        out_shape=(
            jax.ShapeDtypeStruct((down.shape[0], down.shape[1] * count), down.dtype),
            jax.ShapeDtypeStruct((up.shape[0] * count, up.shape[1]), up.dtype),
        ),
        in_specs=[pl.BlockSpec(memory_space=pltpu.VMEM)] * 2,
        out_specs=(pl.BlockSpec(memory_space=pl.ANY), pl.BlockSpec(memory_space=pl.ANY)),
        scratch_shapes=[pltpu.SemaphoreType.DMA((6,))],
        compiler_params=pltpu.CompilerParams(collective_id=5, has_side_effects=True),
    )(down, up)


def on_device(
    tokens,
    cotangent,
    expert_ids,
    slot_ids,
    gate_weights,
    latent_down,
    latent_up,
    expert_gate,
    expert_linear,
    expert_out,
):
    row_count = tokens.shape[0]
    pick_count = expert_ids.shape[1]
    local_count = expert_gate.shape[0]
    group_count = lax.axis_size("expert")
    expert_count = group_count * local_count
    capacity = min(
        row_count, 2 * ((9 * row_count * pick_count + 16 * expert_count - 1) // (16 * expert_count))
    )
    down_full, up_full = dp_gather(latent_down, latent_up)
    gate_full, linear_full, output_full = (
        lax.all_gather(expert_gate, "dp", axis=1, tiled=True),
        lax.all_gather(expert_linear, "dp", axis=1, tiled=True),
        lax.all_gather(expert_out, "dp", axis=2, tiled=True),
    )
    latent_part = jnp.dot(tokens, down_full, preferred_element_type=jnp.float32)
    back_part = lax.dot_general(
        cotangent, up_full, (((1,), (1,)), ((), ())), preferred_element_type=jnp.float32
    )
    width = latent_part.shape[1]
    swap = [(0, 1), (1, 0)]
    latent_mine = latent_part.astype(jnp.bfloat16)
    latent_other = lax.ppermute(latent_mine, "half", swap)
    back_mine = back_part.astype(jnp.bfloat16)
    back_other = lax.ppermute(back_mine, "half", swap)
    latent = (latent_mine.astype(jnp.float32) + latent_other.astype(jnp.float32)).astype(jnp.bfloat16)
    back_latent = back_mine.astype(jnp.float32) + back_other.astype(jnp.float32)
    half_cap = capacity // 2
    side = lax.axis_index("half")
    swap = [(0, 1), (1, 0)]
    flat_slot = (expert_ids * capacity + slot_ids).reshape(-1)
    owned_shape = (expert_count, half_cap)
    owned_slot = (
        lax.broadcasted_iota(jnp.int32, owned_shape, 0) * capacity
        + side * half_cap
        + lax.broadcasted_iota(jnp.int32, owned_shape, 1)
    ).reshape(-1)
    matches = (flat_slot[None, :] == owned_slot[:, None]).reshape(-1, row_count, pick_count)
    picks = jnp.any(matches, axis=2).astype(jnp.bfloat16)
    weights = jnp.sum(jnp.where(matches, gate_weights[None], 0.0), axis=2)
    send_latent = jnp.dot(picks, latent, preferred_element_type=jnp.float32).astype(jnp.bfloat16)
    send_back = jnp.dot(
        weights,
        back_latent,
        precision=lax.Precision.HIGHEST,
        preferred_element_type=jnp.float32,
    ).astype(jnp.bfloat16)
    block_shape = (group_count, local_count, half_cap, width)
    mine_latent = all_to_all_kernel(send_latent.reshape(block_shape), 3)
    theirs_latent = lax.ppermute(mine_latent, "half", swap)
    mine_back = all_to_all_kernel(send_back.reshape(block_shape), 6)
    theirs_back = lax.ppermute(mine_back, "half", swap)
    mine = (mine_latent, mine_back)
    theirs = (theirs_latent, theirs_back)

    def forward(rows):
        rows_latent, rows_back = rows
        pre_gate = jnp.einsum(
            "neci,eih->nech", rows_latent, gate_full, preferred_element_type=jnp.float32
        )
        pre_linear = jnp.einsum(
            "neci,eih->nech", rows_latent, linear_full, preferred_element_type=jnp.float32
        )
        grad_hidden = jnp.einsum(
            "necj,ehj->nech", rows_back, output_full, preferred_element_type=jnp.float32
        )
        logistic = jax.nn.sigmoid(pre_gate)
        hidden = (pre_gate * logistic * pre_linear).astype(jnp.bfloat16)
        gate_delta = (
            grad_hidden * pre_linear * logistic * (1.0 + pre_gate * (1.0 - logistic))
        ).astype(jnp.bfloat16)
        linear_delta = (grad_hidden * pre_gate * logistic).astype(jnp.bfloat16)
        return rows_latent, rows_back, hidden, gate_delta, linear_delta

    def row_grad(gate_delta, linear_delta):
        row_part = jnp.einsum(
            "nech,eih->neci", gate_delta, gate_full, preferred_element_type=jnp.float32
        )
        return row_part + jnp.einsum(
            "nech,eih->neci", linear_delta, linear_full, preferred_element_type=jnp.float32
        )

    def weight_grads(rows_latent, rows_back, hidden, gate_delta, linear_delta):
        gate_part = jnp.einsum(
            "neci,nech->eih", rows_latent, gate_delta, preferred_element_type=jnp.float32
        )
        linear_part = jnp.einsum(
            "neci,nech->eih", rows_latent, linear_delta, preferred_element_type=jnp.float32
        )
        out_part = jnp.einsum(
            "nech,necj->ehj", hidden, rows_back, preferred_element_type=jnp.float32
        )
        return gate_part, linear_part, out_part

    own = forward(mine)
    own_row = row_grad(own[3], own[4])
    own_parts = weight_grads(*own)
    theirs, own_row, own_parts = lax.optimization_barrier((theirs, own_row, own_parts))
    other = forward(theirs)
    send_rows = row_grad(other[3], other[4]).astype(jnp.bfloat16)
    send_rows, other = lax.optimization_barrier((send_rows, other))
    other_rows = lax.ppermute(send_rows, "half", swap)
    other_parts = weight_grads(*other)
    parts = tuple((a + b).astype(jnp.bfloat16) for a, b in zip(own_parts, other_parts))
    other_rows, parts = lax.optimization_barrier((other_rows, parts))
    own_rows = own_row + other_rows.astype(jnp.float32)
    gate_part, linear_part, out_part = parts
    gate_share, linear_share, out_share = (
        lax.psum_scatter(
            gate_part.astype(jnp.bfloat16), "dp", scatter_dimension=1, tiled=True
        ).astype(jnp.float32),
        lax.psum_scatter(
            linear_part.astype(jnp.bfloat16), "dp", scatter_dimension=1, tiled=True
        ).astype(jnp.float32),
        lax.psum_scatter(
            out_part.astype(jnp.bfloat16), "dp", scatter_dimension=2, tiled=True
        ).astype(jnp.float32),
    )
    returned = all_to_all_kernel(own_rows.astype(jnp.bfloat16), 4)
    slot_rel = slot_ids - side * half_cap
    owned = (slot_rel >= 0) & (slot_rel < half_cap)
    position = jnp.where(owned, expert_ids * half_cap + slot_rel, -1).reshape(-1)
    slot_index = lax.broadcasted_iota(jnp.int32, (row_count * pick_count, expert_count * half_cap), 1)
    combine = (position[:, None] == slot_index).reshape(row_count, pick_count, -1)
    combine = jnp.any(combine, axis=1).astype(jnp.bfloat16)
    latent_half = jnp.dot(
        combine,
        returned.reshape(expert_count * half_cap, width),
        preferred_element_type=jnp.float32,
    )
    latent_grad = pair_sum(latent_half, 2)
    token_grad = lax.dot_general(
        latent_grad.astype(jnp.bfloat16),
        down_full,
        (((1,), (1,)), ((), ())),
        preferred_element_type=jnp.float32,
    )
    return (
        token_grad.astype(jnp.bfloat16),
        gate_share.astype(jnp.bfloat16),
        linear_share.astype(jnp.bfloat16),
        out_share.astype(jnp.bfloat16),
    )


def solution(mesh):
    in_specs = (
        P(("expert", "dp"), "half"),
        P(("expert", "dp"), "half"),
        P(("expert", "dp"), None),
        P(("expert", "dp"), None),
        P(("expert", "dp"), None),
        P("half", "dp"),
        P("dp", "half"),
        P("expert", "dp", "half"),
        P("expert", "dp", "half"),
        P("expert", "half", "dp"),
    )
    out_specs = (
        P(("expert", "dp"), "half"),
        P("expert", "dp", "half"),
        P("expert", "dp", "half"),
        P("expert", "half", "dp"),
    )
    return jax.shard_map(
        on_device, mesh=mesh, in_specs=in_specs, out_specs=out_specs, check_vma=False
    )
```

```python
import functools

import jax
import jax.numpy as jnp
from jax import lax
from jax.experimental import pallas as pl
from jax.experimental.pallas import tpu as pltpu
from jax.sharding import PartitionSpec as P

MESH = pl.DeviceIdType.MESH


def _pair_sum_kernel(x_ref, o_ref, buf, send_sem, recv_sem):
    other = 1 - lax.axis_index("half")
    barrier = pltpu.get_barrier_semaphore()
    pl.semaphore_signal(barrier, inc=1, device_id={"half": other}, device_id_type=MESH)
    pl.semaphore_wait(barrier, 1)
    copy = pltpu.make_async_remote_copy(
        src_ref=x_ref,
        dst_ref=buf,
        send_sem=send_sem,
        recv_sem=recv_sem,
        device_id={"half": other},
        device_id_type=MESH,
    )
    copy.start()
    copy.wait()
    o_ref[...] = x_ref[...].astype(jnp.float32) + buf[...].astype(jnp.float32)


def pair_sum(x, collective_id):
    x = x.astype(jnp.bfloat16)
    return pl.pallas_call(
        _pair_sum_kernel,
        out_shape=jax.ShapeDtypeStruct(x.shape, jnp.float32),
        in_specs=[pl.BlockSpec(memory_space=pltpu.VMEM)],
        out_specs=pl.BlockSpec(memory_space=pltpu.VMEM),
        scratch_shapes=[
            pltpu.VMEM(x.shape, x.dtype),
            pltpu.SemaphoreType.DMA(()),
            pltpu.SemaphoreType.DMA(()),
        ],
        compiler_params=pltpu.CompilerParams(collective_id=collective_id, has_side_effects=True),
    )(x)


def _all_to_all_kernel(x_ref, o_ref, send_sem, recv_sem, local_sem):
    count = x_ref.shape[0]
    me = lax.axis_index("expert")
    barrier = pltpu.get_barrier_semaphore()

    def greet(step, carry):
        peer = lax.rem(me + step, count)
        pl.semaphore_signal(barrier, inc=1, device_id={"expert": peer}, device_id_type=MESH)
        return carry

    lax.fori_loop(1, count, greet, 0)
    pl.semaphore_wait(barrier, count - 1)
    local = pltpu.make_async_copy(x_ref.at[me], o_ref.at[me], local_sem)
    local.start()

    def remote(peer):
        return pltpu.make_async_remote_copy(
            src_ref=x_ref.at[peer],
            dst_ref=o_ref.at[me],
            send_sem=send_sem.at[peer],
            recv_sem=recv_sem.at[me],
            device_id={"expert": peer},
            device_id_type=MESH,
        )

    def send(step, carry):
        offset = lax.select(step % 2 == 1, (step + 1) // 2, count - step // 2)
        remote(lax.rem(me + offset, count)).start()
        return carry

    lax.fori_loop(1, count, send, 0)

    def drain(step, carry):
        peer = lax.rem(me + step, count)
        remote(peer).wait_send()
        pltpu.make_async_remote_copy(
            src_ref=x_ref.at[peer],
            dst_ref=o_ref.at[peer],
            send_sem=send_sem.at[peer],
            recv_sem=recv_sem.at[peer],
            device_id={"expert": peer},
            device_id_type=MESH,
        ).wait_recv()
        return carry

    lax.fori_loop(1, count, drain, 0)
    local.wait()


def all_to_all_kernel(x, collective_id):
    count = lax.axis_size("expert")
    shape = x.shape
    blocks = x.reshape(count, -1, shape[-1])
    out = pl.pallas_call(
        _all_to_all_kernel,
        out_shape=jax.ShapeDtypeStruct(blocks.shape, blocks.dtype),
        in_specs=[pl.BlockSpec(memory_space=pl.ANY)],
        out_specs=pl.BlockSpec(memory_space=pl.ANY),
        scratch_shapes=[
            pltpu.SemaphoreType.DMA((count,)),
            pltpu.SemaphoreType.DMA((count,)),
            pltpu.SemaphoreType.DMA(()),
        ],
        compiler_params=pltpu.CompilerParams(collective_id=collective_id, has_side_effects=True),
    )(blocks)
    return out.reshape(shape)


def _dp_gather_kernel(down_ref, up_ref, down_out, up_out, sems):
    me = lax.axis_index("dp")
    other = 1 - me
    barrier = pltpu.get_barrier_semaphore()
    pl.semaphore_signal(barrier, inc=1, device_id={"dp": other}, device_id_type=MESH)
    pl.semaphore_wait(barrier, 1)
    cols = down_ref.shape[1]
    rows = up_ref.shape[0]
    down_dst = down_out.at[:, pl.ds(pl.multiple_of(me * cols, cols), cols)]
    up_dst = up_out.at[pl.ds(pl.multiple_of(me * rows, rows), rows), :]
    copies = [
        pltpu.make_async_remote_copy(
            src_ref=down_ref,
            dst_ref=down_dst,
            send_sem=sems.at[0],
            recv_sem=sems.at[1],
            device_id={"dp": other},
            device_id_type=MESH,
        ),
        pltpu.make_async_remote_copy(
            src_ref=up_ref,
            dst_ref=up_dst,
            send_sem=sems.at[2],
            recv_sem=sems.at[3],
            device_id={"dp": other},
            device_id_type=MESH,
        ),
        pltpu.make_async_copy(down_ref, down_dst, sems.at[4]),
        pltpu.make_async_copy(up_ref, up_dst, sems.at[5]),
    ]
    for copy in copies:
        copy.start()
    for copy in copies:
        copy.wait()


def dp_gather(down, up):
    count = lax.axis_size("dp")
    return pl.pallas_call(
        _dp_gather_kernel,
        out_shape=(
            jax.ShapeDtypeStruct((down.shape[0], down.shape[1] * count), down.dtype),
            jax.ShapeDtypeStruct((up.shape[0] * count, up.shape[1]), up.dtype),
        ),
        in_specs=[pl.BlockSpec(memory_space=pltpu.VMEM)] * 2,
        out_specs=(pl.BlockSpec(memory_space=pl.ANY), pl.BlockSpec(memory_space=pl.ANY)),
        scratch_shapes=[pltpu.SemaphoreType.DMA((6,))],
        compiler_params=pltpu.CompilerParams(collective_id=5, has_side_effects=True),
    )(down, up)


def on_device(
    tokens,
    cotangent,
    expert_ids,
    slot_ids,
    gate_weights,
    latent_down,
    latent_up,
    expert_gate,
    expert_linear,
    expert_out,
):
    row_count = tokens.shape[0]
    pick_count = expert_ids.shape[1]
    local_count = expert_gate.shape[0]
    group_count = lax.axis_size("expert")
    expert_count = group_count * local_count
    capacity = min(
        row_count, 2 * ((9 * row_count * pick_count + 16 * expert_count - 1) // (16 * expert_count))
    )
    down_full, up_full = dp_gather(latent_down, latent_up)
    gate_full, linear_full, output_full = (
        lax.all_gather(expert_gate, "dp", axis=1, tiled=True),
        lax.all_gather(expert_linear, "dp", axis=1, tiled=True),
        lax.all_gather(expert_out, "dp", axis=2, tiled=True),
    )
    latent_part = jnp.dot(tokens, down_full, preferred_element_type=jnp.float32)
    back_part = lax.dot_general(
        cotangent, up_full, (((1,), (1,)), ((), ())), preferred_element_type=jnp.float32
    )
    width = latent_part.shape[1]
    both = pair_sum(jnp.concatenate([latent_part, back_part], axis=1), 1)
    latent = both[:, :width].astype(jnp.bfloat16)
    back_latent = both[:, width:]
    half_cap = capacity // 2
    side = lax.axis_index("half")
    swap = [(0, 1), (1, 0)]
    flat_slot = (expert_ids * capacity + slot_ids).reshape(-1)
    owned_shape = (expert_count, half_cap)
    owned_slot = (
        lax.broadcasted_iota(jnp.int32, owned_shape, 0) * capacity
        + side * half_cap
        + lax.broadcasted_iota(jnp.int32, owned_shape, 1)
    ).reshape(-1)
    matches = (flat_slot[None, :] == owned_slot[:, None]).reshape(-1, row_count, pick_count)
    picks = jnp.any(matches, axis=2).astype(jnp.bfloat16)
    weights = jnp.sum(jnp.where(matches, gate_weights[None], 0.0), axis=2)
    send_latent = jnp.dot(picks, latent, preferred_element_type=jnp.float32).astype(jnp.bfloat16)
    send_back = jnp.dot(
        weights,
        back_latent,
        precision=lax.Precision.HIGHEST,
        preferred_element_type=jnp.float32,
    ).astype(jnp.bfloat16)
    block_shape = (group_count, local_count, half_cap, width)
    mine_latent = all_to_all_kernel(send_latent.reshape(block_shape), 3)
    theirs_latent = lax.ppermute(mine_latent, "half", swap)
    mine_back = all_to_all_kernel(send_back.reshape(block_shape), 6)
    theirs_back = lax.ppermute(mine_back, "half", swap)
    mine = (mine_latent, mine_back)
    theirs = (theirs_latent, theirs_back)

    def forward(rows):
        rows_latent, rows_back = rows
        pre_gate = jnp.einsum(
            "neci,eih->nech", rows_latent, gate_full, preferred_element_type=jnp.float32
        )
        pre_linear = jnp.einsum(
            "neci,eih->nech", rows_latent, linear_full, preferred_element_type=jnp.float32
        )
        grad_hidden = jnp.einsum(
            "necj,ehj->nech", rows_back, output_full, preferred_element_type=jnp.float32
        )
        logistic = jax.nn.sigmoid(pre_gate)
        hidden = (pre_gate * logistic * pre_linear).astype(jnp.bfloat16)
        gate_delta = (
            grad_hidden * pre_linear * logistic * (1.0 + pre_gate * (1.0 - logistic))
        ).astype(jnp.bfloat16)
        linear_delta = (grad_hidden * pre_gate * logistic).astype(jnp.bfloat16)
        return rows_latent, rows_back, hidden, gate_delta, linear_delta

    def row_grad(gate_delta, linear_delta):
        row_part = jnp.einsum(
            "nech,eih->neci", gate_delta, gate_full, preferred_element_type=jnp.float32
        )
        return row_part + jnp.einsum(
            "nech,eih->neci", linear_delta, linear_full, preferred_element_type=jnp.float32
        )

    def weight_grads(rows_latent, rows_back, hidden, gate_delta, linear_delta):
        gate_part = jnp.einsum(
            "neci,nech->eih", rows_latent, gate_delta, preferred_element_type=jnp.float32
        )
        linear_part = jnp.einsum(
            "neci,nech->eih", rows_latent, linear_delta, preferred_element_type=jnp.float32
        )
        out_part = jnp.einsum(
            "nech,necj->ehj", hidden, rows_back, preferred_element_type=jnp.float32
        )
        return gate_part, linear_part, out_part

    own = forward(mine)
    own_row = row_grad(own[3], own[4])
    own_parts = weight_grads(*own)
    theirs, own_row, own_parts = lax.optimization_barrier((theirs, own_row, own_parts))
    other = forward(theirs)
    send_rows = row_grad(other[3], other[4]).astype(jnp.bfloat16)
    send_rows, other = lax.optimization_barrier((send_rows, other))
    other_rows = lax.ppermute(send_rows, "half", swap)
    other_parts = weight_grads(*other)
    parts = tuple((a + b).astype(jnp.bfloat16) for a, b in zip(own_parts, other_parts))
    other_rows, parts = lax.optimization_barrier((other_rows, parts))
    own_rows = own_row + other_rows.astype(jnp.float32)
    gate_part, linear_part, out_part = parts
    gate_share, linear_share, out_share = (
        lax.psum_scatter(
            gate_part.astype(jnp.bfloat16), "dp", scatter_dimension=1, tiled=True
        ).astype(jnp.float32),
        lax.psum_scatter(
            linear_part.astype(jnp.bfloat16), "dp", scatter_dimension=1, tiled=True
        ).astype(jnp.float32),
        lax.psum_scatter(
            out_part.astype(jnp.bfloat16), "dp", scatter_dimension=2, tiled=True
        ).astype(jnp.float32),
    )
    returned = all_to_all_kernel(own_rows.astype(jnp.bfloat16), 4)
    slot_rel = slot_ids - side * half_cap
    owned = (slot_rel >= 0) & (slot_rel < half_cap)
    position = jnp.where(owned, expert_ids * half_cap + slot_rel, -1).reshape(-1)
    slot_index = lax.broadcasted_iota(jnp.int32, (row_count * pick_count, expert_count * half_cap), 1)
    combine = (position[:, None] == slot_index).reshape(row_count, pick_count, -1)
    combine = jnp.any(combine, axis=1).astype(jnp.bfloat16)
    latent_half = jnp.dot(
        combine,
        returned.reshape(expert_count * half_cap, width),
        preferred_element_type=jnp.float32,
    )
    latent_grad = pair_sum(latent_half, 2)
    token_grad = lax.dot_general(
        latent_grad.astype(jnp.bfloat16),
        down_full,
        (((1,), (1,)), ((), ())),
        preferred_element_type=jnp.float32,
    )
    return (
        token_grad.astype(jnp.bfloat16),
        gate_share.astype(jnp.bfloat16),
        linear_share.astype(jnp.bfloat16),
        out_share.astype(jnp.bfloat16),
    )


def solution(mesh):
    in_specs = (
        P(("expert", "dp"), "half"),
        P(("expert", "dp"), "half"),
        P(("expert", "dp"), None),
        P(("expert", "dp"), None),
        P(("expert", "dp"), None),
        P("half", "dp"),
        P("dp", "half"),
        P("expert", "dp", "half"),
        P("expert", "dp", "half"),
        P("expert", "half", "dp"),
    )
    out_specs = (
        P(("expert", "dp"), "half"),
        P("expert", "dp", "half"),
        P("expert", "dp", "half"),
        P("expert", "half", "dp"),
    )
    return jax.shard_map(
        on_device, mesh=mesh, in_specs=in_specs, out_specs=out_specs, check_vma=False
    )
```

```python
import functools

import jax
import jax.numpy as jnp
from jax import lax
from jax.experimental import pallas as pl
from jax.experimental.pallas import tpu as pltpu
from jax.sharding import PartitionSpec as P

MESH = pl.DeviceIdType.MESH


def _pair_sum_kernel(x_ref, o_ref, buf, send_sem, recv_sem):
    other = 1 - lax.axis_index("half")
    barrier = pltpu.get_barrier_semaphore()
    pl.semaphore_signal(barrier, inc=1, device_id={"half": other}, device_id_type=MESH)
    pl.semaphore_wait(barrier, 1)
    copy = pltpu.make_async_remote_copy(
        src_ref=x_ref,
        dst_ref=buf,
        send_sem=send_sem,
        recv_sem=recv_sem,
        device_id={"half": other},
        device_id_type=MESH,
    )
    copy.start()
    copy.wait()
    o_ref[...] = x_ref[...].astype(jnp.float32) + buf[...].astype(jnp.float32)


def pair_sum(x, collective_id):
    x = x.astype(jnp.bfloat16)
    return pl.pallas_call(
        _pair_sum_kernel,
        out_shape=jax.ShapeDtypeStruct(x.shape, jnp.float32),
        in_specs=[pl.BlockSpec(memory_space=pltpu.VMEM)],
        out_specs=pl.BlockSpec(memory_space=pltpu.VMEM),
        scratch_shapes=[
            pltpu.VMEM(x.shape, x.dtype),
            pltpu.SemaphoreType.DMA(()),
            pltpu.SemaphoreType.DMA(()),
        ],
        compiler_params=pltpu.CompilerParams(collective_id=collective_id, has_side_effects=True),
    )(x)


def _all_to_all_kernel(x_ref, o_ref, send_sem, recv_sem, local_sem):
    count = x_ref.shape[0]
    me = lax.axis_index("expert")
    barrier = pltpu.get_barrier_semaphore()

    def greet(step, carry):
        peer = lax.rem(me + step, count)
        pl.semaphore_signal(barrier, inc=1, device_id={"expert": peer}, device_id_type=MESH)
        return carry

    lax.fori_loop(1, count, greet, 0)
    pl.semaphore_wait(barrier, count - 1)
    local = pltpu.make_async_copy(x_ref.at[me], o_ref.at[me], local_sem)
    local.start()

    def remote(peer):
        return pltpu.make_async_remote_copy(
            src_ref=x_ref.at[peer],
            dst_ref=o_ref.at[me],
            send_sem=send_sem.at[peer],
            recv_sem=recv_sem.at[me],
            device_id={"expert": peer},
            device_id_type=MESH,
        )

    def send(step, carry):
        remote(lax.rem(me + step, count)).start()
        return carry

    lax.fori_loop(1, count, send, 0)

    def drain(step, carry):
        peer = lax.rem(me + step, count)
        remote(peer).wait_send()
        pltpu.make_async_remote_copy(
            src_ref=x_ref.at[peer],
            dst_ref=o_ref.at[peer],
            send_sem=send_sem.at[peer],
            recv_sem=recv_sem.at[peer],
            device_id={"expert": peer},
            device_id_type=MESH,
        ).wait_recv()
        return carry

    lax.fori_loop(1, count, drain, 0)
    local.wait()


def all_to_all_kernel(x, collective_id):
    count = lax.axis_size("expert")
    shape = x.shape
    blocks = x.reshape(count, -1, 128)
    out = pl.pallas_call(
        _all_to_all_kernel,
        out_shape=jax.ShapeDtypeStruct(blocks.shape, blocks.dtype),
        in_specs=[pl.BlockSpec(memory_space=pl.ANY)],
        out_specs=pl.BlockSpec(memory_space=pl.ANY),
        scratch_shapes=[
            pltpu.SemaphoreType.DMA((count,)),
            pltpu.SemaphoreType.DMA((count,)),
            pltpu.SemaphoreType.DMA(()),
        ],
        compiler_params=pltpu.CompilerParams(collective_id=collective_id, has_side_effects=True),
    )(blocks)
    return out.reshape(shape)


def _dp_gather_kernel(down_ref, up_ref, down_out, up_out, sems):
    me = lax.axis_index("dp")
    other = 1 - me
    barrier = pltpu.get_barrier_semaphore()
    pl.semaphore_signal(barrier, inc=1, device_id={"dp": other}, device_id_type=MESH)
    pl.semaphore_wait(barrier, 1)
    cols = down_ref.shape[1]
    rows = up_ref.shape[0]
    down_dst = down_out.at[:, pl.ds(pl.multiple_of(me * cols, cols), cols)]
    up_dst = up_out.at[pl.ds(pl.multiple_of(me * rows, rows), rows), :]
    copies = [
        pltpu.make_async_remote_copy(
            src_ref=down_ref,
            dst_ref=down_dst,
            send_sem=sems.at[0],
            recv_sem=sems.at[1],
            device_id={"dp": other},
            device_id_type=MESH,
        ),
        pltpu.make_async_remote_copy(
            src_ref=up_ref,
            dst_ref=up_dst,
            send_sem=sems.at[2],
            recv_sem=sems.at[3],
            device_id={"dp": other},
            device_id_type=MESH,
        ),
        pltpu.make_async_copy(down_ref, down_dst, sems.at[4]),
        pltpu.make_async_copy(up_ref, up_dst, sems.at[5]),
    ]
    for copy in copies:
        copy.start()
    for copy in copies:
        copy.wait()


def dp_gather(down, up):
    count = lax.axis_size("dp")
    return pl.pallas_call(
        _dp_gather_kernel,
        out_shape=(
            jax.ShapeDtypeStruct((down.shape[0], down.shape[1] * count), down.dtype),
            jax.ShapeDtypeStruct((up.shape[0] * count, up.shape[1]), up.dtype),
        ),
        in_specs=[pl.BlockSpec(memory_space=pltpu.VMEM)] * 2,
        out_specs=(pl.BlockSpec(memory_space=pl.ANY), pl.BlockSpec(memory_space=pl.ANY)),
        scratch_shapes=[pltpu.SemaphoreType.DMA((6,))],
        compiler_params=pltpu.CompilerParams(collective_id=5, has_side_effects=True),
    )(down, up)


def on_device(
    tokens,
    cotangent,
    expert_ids,
    slot_ids,
    gate_weights,
    latent_down,
    latent_up,
    expert_gate,
    expert_linear,
    expert_out,
):
    row_count = tokens.shape[0]
    pick_count = expert_ids.shape[1]
    local_count = expert_gate.shape[0]
    group_count = lax.axis_size("expert")
    expert_count = group_count * local_count
    capacity = min(
        row_count, 2 * ((9 * row_count * pick_count + 16 * expert_count - 1) // (16 * expert_count))
    )
    down_full, up_full = dp_gather(latent_down, latent_up)
    gate_full, linear_full, output_full = (
        lax.all_gather(expert_gate, "dp", axis=1, tiled=True),
        lax.all_gather(expert_linear, "dp", axis=1, tiled=True),
        lax.all_gather(expert_out, "dp", axis=2, tiled=True),
    )
    latent_part = jnp.dot(tokens, down_full, preferred_element_type=jnp.float32)
    back_part = lax.dot_general(
        cotangent, up_full, (((1,), (1,)), ((), ())), preferred_element_type=jnp.float32
    )
    width = latent_part.shape[1]
    both = pair_sum(jnp.concatenate([latent_part, back_part], axis=1), 1)
    latent = both[:, :width].astype(jnp.bfloat16)
    back_latent = both[:, width:]
    half_cap = capacity // 2
    side = lax.axis_index("half")
    swap = [(0, 1), (1, 0)]
    flat_slot = (expert_ids * capacity + slot_ids).reshape(-1)
    owned_shape = (expert_count, half_cap)
    owned_slot = (
        lax.broadcasted_iota(jnp.int32, owned_shape, 0) * capacity
        + side * half_cap
        + lax.broadcasted_iota(jnp.int32, owned_shape, 1)
    ).reshape(-1)
    matches = (flat_slot[None, :] == owned_slot[:, None]).reshape(-1, row_count, pick_count)
    picks = jnp.any(matches, axis=2).astype(jnp.bfloat16)
    weights = jnp.sum(jnp.where(matches, gate_weights[None], 0.0), axis=2)
    send_latent = jnp.dot(picks, latent, preferred_element_type=jnp.float32).astype(jnp.bfloat16)
    send_back = jnp.dot(
        weights,
        back_latent,
        precision=lax.Precision.HIGHEST,
        preferred_element_type=jnp.float32,
    ).astype(jnp.bfloat16)
    block_shape = (group_count, local_count, half_cap, width)
    mine_latent = all_to_all_kernel(send_latent.reshape(block_shape), 3)
    theirs_latent = lax.ppermute(mine_latent, "half", swap)
    mine_back = all_to_all_kernel(send_back.reshape(block_shape), 6)
    theirs_back = lax.ppermute(mine_back, "half", swap)
    mine = (mine_latent, mine_back)
    theirs = (theirs_latent, theirs_back)

    def forward(rows):
        rows_latent, rows_back = rows
        pre_gate = jnp.einsum(
            "neci,eih->nech", rows_latent, gate_full, preferred_element_type=jnp.float32
        )
        pre_linear = jnp.einsum(
            "neci,eih->nech", rows_latent, linear_full, preferred_element_type=jnp.float32
        )
        grad_hidden = jnp.einsum(
            "necj,ehj->nech", rows_back, output_full, preferred_element_type=jnp.float32
        )
        logistic = jax.nn.sigmoid(pre_gate)
        hidden = (pre_gate * logistic * pre_linear).astype(jnp.bfloat16)
        gate_delta = (
            grad_hidden * pre_linear * logistic * (1.0 + pre_gate * (1.0 - logistic))
        ).astype(jnp.bfloat16)
        linear_delta = (grad_hidden * pre_gate * logistic).astype(jnp.bfloat16)
        return rows_latent, rows_back, hidden, gate_delta, linear_delta

    def row_grad(gate_delta, linear_delta):
        row_part = jnp.einsum(
            "nech,eih->neci", gate_delta, gate_full, preferred_element_type=jnp.float32
        )
        return row_part + jnp.einsum(
            "nech,eih->neci", linear_delta, linear_full, preferred_element_type=jnp.float32
        )

    def weight_grads(rows_latent, rows_back, hidden, gate_delta, linear_delta):
        gate_part = jnp.einsum(
            "neci,nech->eih", rows_latent, gate_delta, preferred_element_type=jnp.float32
        )
        linear_part = jnp.einsum(
            "neci,nech->eih", rows_latent, linear_delta, preferred_element_type=jnp.float32
        )
        out_part = jnp.einsum(
            "nech,necj->ehj", hidden, rows_back, preferred_element_type=jnp.float32
        )
        return gate_part, linear_part, out_part

    own = forward(mine)
    own_row = row_grad(own[3], own[4])
    own_parts = weight_grads(*own)
    theirs, own_row, own_parts = lax.optimization_barrier((theirs, own_row, own_parts))
    other = forward(theirs)
    send_rows = row_grad(other[3], other[4]).astype(jnp.bfloat16)
    send_rows, other = lax.optimization_barrier((send_rows, other))
    other_rows = lax.ppermute(send_rows, "half", swap)
    other_parts = weight_grads(*other)
    parts = tuple((a + b).astype(jnp.bfloat16) for a, b in zip(own_parts, other_parts))
    other_rows, parts = lax.optimization_barrier((other_rows, parts))
    own_rows = own_row + other_rows.astype(jnp.float32)
    gate_part, linear_part, out_part = parts
    gate_share, linear_share, out_share = (
        lax.psum_scatter(
            gate_part.astype(jnp.bfloat16), "dp", scatter_dimension=1, tiled=True
        ).astype(jnp.float32),
        lax.psum_scatter(
            linear_part.astype(jnp.bfloat16), "dp", scatter_dimension=1, tiled=True
        ).astype(jnp.float32),
        lax.psum_scatter(
            out_part.astype(jnp.bfloat16), "dp", scatter_dimension=2, tiled=True
        ).astype(jnp.float32),
    )
    returned = all_to_all_kernel(own_rows.astype(jnp.bfloat16), 4)
    slot_rel = slot_ids - side * half_cap
    owned = (slot_rel >= 0) & (slot_rel < half_cap)
    position = jnp.where(owned, expert_ids * half_cap + slot_rel, -1).reshape(-1)
    slot_index = lax.broadcasted_iota(jnp.int32, (row_count * pick_count, expert_count * half_cap), 1)
    combine = (position[:, None] == slot_index).reshape(row_count, pick_count, -1)
    combine = jnp.any(combine, axis=1).astype(jnp.bfloat16)
    latent_half = jnp.dot(
        combine,
        returned.reshape(expert_count * half_cap, width),
        preferred_element_type=jnp.float32,
    )
    latent_grad = pair_sum(latent_half, 2)
    token_grad = lax.dot_general(
        latent_grad.astype(jnp.bfloat16),
        down_full,
        (((1,), (1,)), ((), ())),
        preferred_element_type=jnp.float32,
    )
    return (
        token_grad.astype(jnp.bfloat16),
        gate_share.astype(jnp.bfloat16),
        linear_share.astype(jnp.bfloat16),
        out_share.astype(jnp.bfloat16),
    )


def solution(mesh):
    in_specs = (
        P(("expert", "dp"), "half"),
        P(("expert", "dp"), "half"),
        P(("expert", "dp"), None),
        P(("expert", "dp"), None),
        P(("expert", "dp"), None),
        P("half", "dp"),
        P("dp", "half"),
        P("expert", "dp", "half"),
        P("expert", "dp", "half"),
        P("expert", "half", "dp"),
    )
    out_specs = (
        P(("expert", "dp"), "half"),
        P("expert", "dp", "half"),
        P("expert", "dp", "half"),
        P("expert", "half", "dp"),
    )
    return jax.shard_map(
        on_device, mesh=mesh, in_specs=in_specs, out_specs=out_specs, check_vma=False
    )
```

```python
import functools

import jax
import jax.numpy as jnp
from jax import lax
from jax.experimental import pallas as pl
from jax.experimental.pallas import tpu as pltpu
from jax.sharding import PartitionSpec as P

MESH = pl.DeviceIdType.MESH


def _pair_sum_kernel(x_ref, o_ref, buf, send_sem, recv_sem):
    other = 1 - lax.axis_index("half")
    barrier = pltpu.get_barrier_semaphore()
    pl.semaphore_signal(barrier, inc=1, device_id={"half": other}, device_id_type=MESH)
    pl.semaphore_wait(barrier, 1)
    copy = pltpu.make_async_remote_copy(
        src_ref=x_ref,
        dst_ref=buf,
        send_sem=send_sem,
        recv_sem=recv_sem,
        device_id={"half": other},
        device_id_type=MESH,
    )
    copy.start()
    copy.wait()
    o_ref[...] = x_ref[...].astype(jnp.float32) + buf[...].astype(jnp.float32)


def pair_sum(x, collective_id):
    x = x.astype(jnp.bfloat16)
    return pl.pallas_call(
        _pair_sum_kernel,
        out_shape=jax.ShapeDtypeStruct(x.shape, jnp.float32),
        in_specs=[pl.BlockSpec(memory_space=pltpu.VMEM)],
        out_specs=pl.BlockSpec(memory_space=pltpu.VMEM),
        scratch_shapes=[
            pltpu.VMEM(x.shape, x.dtype),
            pltpu.SemaphoreType.DMA(()),
            pltpu.SemaphoreType.DMA(()),
        ],
        compiler_params=pltpu.CompilerParams(collective_id=collective_id, has_side_effects=True),
    )(x)


def _all_to_all_kernel(x_ref, o_ref, send_sem, recv_sem, local_sem):
    count = x_ref.shape[0]
    me = lax.axis_index("expert")
    barrier = pltpu.get_barrier_semaphore()

    def greet(step, carry):
        peer = lax.rem(me + step, count)
        pl.semaphore_signal(barrier, inc=1, device_id={"expert": peer}, device_id_type=MESH)
        return carry

    lax.fori_loop(1, count, greet, 0)
    pl.semaphore_wait(barrier, count - 1)
    local = pltpu.make_async_copy(x_ref.at[me], o_ref.at[me], local_sem)
    local.start()

    def remote(peer):
        return pltpu.make_async_remote_copy(
            src_ref=x_ref.at[peer],
            dst_ref=o_ref.at[me],
            send_sem=send_sem.at[peer],
            recv_sem=recv_sem.at[me],
            device_id={"expert": peer},
            device_id_type=MESH,
        )

    def send(step, carry):
        remote(lax.rem(me + step, count)).start()
        return carry

    lax.fori_loop(1, count, send, 0)

    def drain(step, carry):
        peer = lax.rem(me + step, count)
        remote(peer).wait_send()
        pltpu.make_async_remote_copy(
            src_ref=x_ref.at[peer],
            dst_ref=o_ref.at[peer],
            send_sem=send_sem.at[peer],
            recv_sem=recv_sem.at[peer],
            device_id={"expert": peer},
            device_id_type=MESH,
        ).wait_recv()
        return carry

    lax.fori_loop(1, count, drain, 0)
    local.wait()


def all_to_all_kernel(x, collective_id):
    count = lax.axis_size("expert")
    shape = x.shape
    blocks = x.reshape(count, -1, 128)
    out = pl.pallas_call(
        _all_to_all_kernel,
        out_shape=jax.ShapeDtypeStruct(blocks.shape, blocks.dtype),
        in_specs=[pl.BlockSpec(memory_space=pl.ANY)],
        out_specs=pl.BlockSpec(memory_space=pl.ANY),
        scratch_shapes=[
            pltpu.SemaphoreType.DMA((count,)),
            pltpu.SemaphoreType.DMA((count,)),
            pltpu.SemaphoreType.DMA(()),
        ],
        compiler_params=pltpu.CompilerParams(collective_id=collective_id, has_side_effects=True),
    )(blocks)
    return out.reshape(shape)


def _dp_gather_kernel(down_ref, up_ref, down_out, up_out, sems):
    me = lax.axis_index("dp")
    other = 1 - me
    barrier = pltpu.get_barrier_semaphore()
    pl.semaphore_signal(barrier, inc=1, device_id={"dp": other}, device_id_type=MESH)
    pl.semaphore_wait(barrier, 1)
    cols = down_ref.shape[1]
    rows = up_ref.shape[0]
    down_dst = down_out.at[:, pl.ds(pl.multiple_of(me * cols, cols), cols)]
    up_dst = up_out.at[pl.ds(pl.multiple_of(me * rows, rows), rows), :]
    copies = [
        pltpu.make_async_remote_copy(
            src_ref=down_ref,
            dst_ref=down_dst,
            send_sem=sems.at[0],
            recv_sem=sems.at[1],
            device_id={"dp": other},
            device_id_type=MESH,
        ),
        pltpu.make_async_remote_copy(
            src_ref=up_ref,
            dst_ref=up_dst,
            send_sem=sems.at[2],
            recv_sem=sems.at[3],
            device_id={"dp": other},
            device_id_type=MESH,
        ),
        pltpu.make_async_copy(down_ref, down_dst, sems.at[4]),
        pltpu.make_async_copy(up_ref, up_dst, sems.at[5]),
    ]
    for copy in copies:
        copy.start()
    for copy in copies:
        copy.wait()


def dp_gather(down, up):
    count = lax.axis_size("dp")
    return pl.pallas_call(
        _dp_gather_kernel,
        out_shape=(
            jax.ShapeDtypeStruct((down.shape[0], down.shape[1] * count), down.dtype),
            jax.ShapeDtypeStruct((up.shape[0] * count, up.shape[1]), up.dtype),
        ),
        in_specs=[pl.BlockSpec(memory_space=pltpu.VMEM)] * 2,
        out_specs=(pl.BlockSpec(memory_space=pl.ANY), pl.BlockSpec(memory_space=pl.ANY)),
        scratch_shapes=[pltpu.SemaphoreType.DMA((6,))],
        compiler_params=pltpu.CompilerParams(collective_id=5, has_side_effects=True),
    )(down, up)


def on_device(
    tokens,
    cotangent,
    expert_ids,
    slot_ids,
    gate_weights,
    latent_down,
    latent_up,
    expert_gate,
    expert_linear,
    expert_out,
):
    row_count = tokens.shape[0]
    pick_count = expert_ids.shape[1]
    local_count = expert_gate.shape[0]
    group_count = lax.axis_size("expert")
    expert_count = group_count * local_count
    capacity = min(
        row_count, 2 * ((9 * row_count * pick_count + 16 * expert_count - 1) // (16 * expert_count))
    )
    down_full, up_full = dp_gather(latent_down, latent_up)
    gate_full, linear_full, output_full = (
        lax.all_gather(expert_gate, "dp", axis=1, tiled=True),
        lax.all_gather(expert_linear, "dp", axis=1, tiled=True),
        lax.all_gather(expert_out, "dp", axis=2, tiled=True),
    )
    latent_part = jnp.dot(tokens, down_full, preferred_element_type=jnp.float32)
    back_part = lax.dot_general(
        cotangent, up_full, (((1,), (1,)), ((), ())), preferred_element_type=jnp.float32
    )
    width = latent_part.shape[1]
    both = pair_sum(jnp.concatenate([latent_part, back_part], axis=1), 1)
    latent = both[:, :width].astype(jnp.bfloat16)
    back_latent = both[:, width:]
    half_cap = capacity // 2
    side = lax.axis_index("half")
    swap = [(0, 1), (1, 0)]
    flat_slot = (expert_ids * capacity + slot_ids).reshape(-1)
    owned_shape = (expert_count, half_cap)
    owned_slot = (
        lax.broadcasted_iota(jnp.int32, owned_shape, 0) * capacity
        + side * half_cap
        + lax.broadcasted_iota(jnp.int32, owned_shape, 1)
    ).reshape(-1)
    matches = (flat_slot[None, :] == owned_slot[:, None]).reshape(-1, row_count, pick_count)
    picks = jnp.any(matches, axis=2).astype(jnp.bfloat16)
    weights = jnp.sum(jnp.where(matches, gate_weights[None], 0.0), axis=2)
    send_latent = jnp.dot(picks, latent, preferred_element_type=jnp.float32).astype(jnp.bfloat16)
    send_back = jnp.dot(
        weights,
        back_latent,
        precision=lax.Precision.HIGHEST,
        preferred_element_type=jnp.float32,
    ).astype(jnp.bfloat16)
    block_shape = (group_count, local_count, half_cap, width)

    def swap_rows(x):
        moved = lax.ppermute(x.reshape(x.shape[0], -1, 128), "half", swap)
        return moved.reshape(x.shape)

    mine_latent = all_to_all_kernel(send_latent.reshape(block_shape), 3)
    theirs_latent = swap_rows(mine_latent)
    mine_back = all_to_all_kernel(send_back.reshape(block_shape), 6)
    theirs_back = swap_rows(mine_back)
    mine = (mine_latent, mine_back)
    theirs = (theirs_latent, theirs_back)

    def forward(rows):
        rows_latent, rows_back = rows
        pre_gate = jnp.einsum(
            "neci,eih->nech", rows_latent, gate_full, preferred_element_type=jnp.float32
        )
        pre_linear = jnp.einsum(
            "neci,eih->nech", rows_latent, linear_full, preferred_element_type=jnp.float32
        )
        grad_hidden = jnp.einsum(
            "necj,ehj->nech", rows_back, output_full, preferred_element_type=jnp.float32
        )
        logistic = jax.nn.sigmoid(pre_gate)
        hidden = (pre_gate * logistic * pre_linear).astype(jnp.bfloat16)
        gate_delta = (
            grad_hidden * pre_linear * logistic * (1.0 + pre_gate * (1.0 - logistic))
        ).astype(jnp.bfloat16)
        linear_delta = (grad_hidden * pre_gate * logistic).astype(jnp.bfloat16)
        return rows_latent, rows_back, hidden, gate_delta, linear_delta

    def row_grad(gate_delta, linear_delta):
        row_part = jnp.einsum(
            "nech,eih->neci", gate_delta, gate_full, preferred_element_type=jnp.float32
        )
        return row_part + jnp.einsum(
            "nech,eih->neci", linear_delta, linear_full, preferred_element_type=jnp.float32
        )

    def weight_grads(rows_latent, rows_back, hidden, gate_delta, linear_delta):
        gate_part = jnp.einsum(
            "neci,nech->eih", rows_latent, gate_delta, preferred_element_type=jnp.float32
        )
        linear_part = jnp.einsum(
            "neci,nech->eih", rows_latent, linear_delta, preferred_element_type=jnp.float32
        )
        out_part = jnp.einsum(
            "nech,necj->ehj", hidden, rows_back, preferred_element_type=jnp.float32
        )
        return gate_part, linear_part, out_part

    own = forward(mine)
    own_row = row_grad(own[3], own[4])
    own_parts = weight_grads(*own)
    theirs, own_row, own_parts = lax.optimization_barrier((theirs, own_row, own_parts))
    other = forward(theirs)
    send_rows = row_grad(other[3], other[4]).astype(jnp.bfloat16)
    send_rows, other = lax.optimization_barrier((send_rows, other))
    other_rows = swap_rows(send_rows)
    other_parts = weight_grads(*other)
    parts = tuple((a + b).astype(jnp.bfloat16) for a, b in zip(own_parts, other_parts))
    other_rows, parts = lax.optimization_barrier((other_rows, parts))
    own_rows = own_row + other_rows.astype(jnp.float32)
    gate_part, linear_part, out_part = parts
    gate_share, linear_share, out_share = (
        lax.psum_scatter(
            gate_part.astype(jnp.bfloat16), "dp", scatter_dimension=1, tiled=True
        ).astype(jnp.float32),
        lax.psum_scatter(
            linear_part.astype(jnp.bfloat16), "dp", scatter_dimension=1, tiled=True
        ).astype(jnp.float32),
        lax.psum_scatter(
            out_part.astype(jnp.bfloat16), "dp", scatter_dimension=2, tiled=True
        ).astype(jnp.float32),
    )
    returned = all_to_all_kernel(own_rows.astype(jnp.bfloat16), 4)
    slot_rel = slot_ids - side * half_cap
    owned = (slot_rel >= 0) & (slot_rel < half_cap)
    position = jnp.where(owned, expert_ids * half_cap + slot_rel, -1).reshape(-1)
    slot_index = lax.broadcasted_iota(jnp.int32, (row_count * pick_count, expert_count * half_cap), 1)
    combine = (position[:, None] == slot_index).reshape(row_count, pick_count, -1)
    combine = jnp.any(combine, axis=1).astype(jnp.bfloat16)
    latent_half = jnp.dot(
        combine,
        returned.reshape(expert_count * half_cap, width),
        preferred_element_type=jnp.float32,
    )
    latent_grad = pair_sum(latent_half, 2)
    token_grad = lax.dot_general(
        latent_grad.astype(jnp.bfloat16),
        down_full,
        (((1,), (1,)), ((), ())),
        preferred_element_type=jnp.float32,
    )
    return (
        token_grad.astype(jnp.bfloat16),
        gate_share.astype(jnp.bfloat16),
        linear_share.astype(jnp.bfloat16),
        out_share.astype(jnp.bfloat16),
    )


def solution(mesh):
    in_specs = (
        P(("expert", "dp"), "half"),
        P(("expert", "dp"), "half"),
        P(("expert", "dp"), None),
        P(("expert", "dp"), None),
        P(("expert", "dp"), None),
        P("half", "dp"),
        P("dp", "half"),
        P("expert", "dp", "half"),
        P("expert", "dp", "half"),
        P("expert", "half", "dp"),
    )
    out_specs = (
        P(("expert", "dp"), "half"),
        P("expert", "dp", "half"),
        P("expert", "dp", "half"),
        P("expert", "half", "dp"),
    )
    return jax.shard_map(
        on_device, mesh=mesh, in_specs=in_specs, out_specs=out_specs, check_vma=False
    )
```

```python
import functools

import jax
import jax.numpy as jnp
from jax import lax
from jax.experimental import pallas as pl
from jax.experimental.pallas import tpu as pltpu
from jax.sharding import PartitionSpec as P

MESH = pl.DeviceIdType.MESH


def _pair_sum_kernel(x_ref, o_ref, buf, send_sem, recv_sem):
    other = 1 - lax.axis_index("half")
    barrier = pltpu.get_barrier_semaphore()
    pl.semaphore_signal(barrier, inc=1, device_id={"half": other}, device_id_type=MESH)
    pl.semaphore_wait(barrier, 1)
    copy = pltpu.make_async_remote_copy(
        src_ref=x_ref,
        dst_ref=buf,
        send_sem=send_sem,
        recv_sem=recv_sem,
        device_id={"half": other},
        device_id_type=MESH,
    )
    copy.start()
    copy.wait()
    o_ref[...] = x_ref[...].astype(jnp.float32) + buf[...].astype(jnp.float32)


def pair_sum(x, collective_id):
    x = x.astype(jnp.bfloat16)
    return pl.pallas_call(
        _pair_sum_kernel,
        out_shape=jax.ShapeDtypeStruct(x.shape, jnp.float32),
        in_specs=[pl.BlockSpec(memory_space=pltpu.VMEM)],
        out_specs=pl.BlockSpec(memory_space=pltpu.VMEM),
        scratch_shapes=[
            pltpu.VMEM(x.shape, x.dtype),
            pltpu.SemaphoreType.DMA(()),
            pltpu.SemaphoreType.DMA(()),
        ],
        compiler_params=pltpu.CompilerParams(collective_id=collective_id, has_side_effects=True),
    )(x)


def _all_to_all_kernel(x_ref, o_ref, send_sem, recv_sem, local_sem):
    count = x_ref.shape[0]
    me = lax.axis_index("expert")
    barrier = pltpu.get_barrier_semaphore()

    def greet(step, carry):
        peer = lax.rem(me + step, count)
        pl.semaphore_signal(barrier, inc=1, device_id={"expert": peer}, device_id_type=MESH)
        return carry

    lax.fori_loop(1, count, greet, 0)
    pl.semaphore_wait(barrier, count - 1)
    local = pltpu.make_async_copy(x_ref.at[me], o_ref.at[me], local_sem)
    local.start()

    def remote(peer):
        return pltpu.make_async_remote_copy(
            src_ref=x_ref.at[peer],
            dst_ref=o_ref.at[me],
            send_sem=send_sem.at[peer],
            recv_sem=recv_sem.at[me],
            device_id={"expert": peer},
            device_id_type=MESH,
        )

    def send(step, carry):
        remote(lax.rem(me + step, count)).start()
        return carry

    lax.fori_loop(1, count, send, 0)

    def drain(step, carry):
        peer = lax.rem(me + step, count)
        remote(peer).wait_send()
        pltpu.make_async_remote_copy(
            src_ref=x_ref.at[peer],
            dst_ref=o_ref.at[peer],
            send_sem=send_sem.at[peer],
            recv_sem=recv_sem.at[peer],
            device_id={"expert": peer},
            device_id_type=MESH,
        ).wait_recv()
        return carry

    lax.fori_loop(1, count, drain, 0)
    local.wait()


def all_to_all_kernel(x, collective_id, keep_blocks=False):
    count = lax.axis_size("expert")
    shape = x.shape
    blocks = x.reshape(count, -1, 128)
    out = pl.pallas_call(
        _all_to_all_kernel,
        out_shape=jax.ShapeDtypeStruct(blocks.shape, blocks.dtype),
        in_specs=[pl.BlockSpec(memory_space=pl.ANY)],
        out_specs=pl.BlockSpec(memory_space=pl.ANY),
        scratch_shapes=[
            pltpu.SemaphoreType.DMA((count,)),
            pltpu.SemaphoreType.DMA((count,)),
            pltpu.SemaphoreType.DMA(()),
        ],
        compiler_params=pltpu.CompilerParams(collective_id=collective_id, has_side_effects=True),
    )(blocks)
    return out if keep_blocks else out.reshape(shape)


def _dp_gather_kernel(down_ref, up_ref, down_out, up_out, sems):
    me = lax.axis_index("dp")
    other = 1 - me
    barrier = pltpu.get_barrier_semaphore()
    pl.semaphore_signal(barrier, inc=1, device_id={"dp": other}, device_id_type=MESH)
    pl.semaphore_wait(barrier, 1)
    cols = down_ref.shape[1]
    rows = up_ref.shape[0]
    down_dst = down_out.at[:, pl.ds(pl.multiple_of(me * cols, cols), cols)]
    up_dst = up_out.at[pl.ds(pl.multiple_of(me * rows, rows), rows), :]
    copies = [
        pltpu.make_async_remote_copy(
            src_ref=down_ref,
            dst_ref=down_dst,
            send_sem=sems.at[0],
            recv_sem=sems.at[1],
            device_id={"dp": other},
            device_id_type=MESH,
        ),
        pltpu.make_async_remote_copy(
            src_ref=up_ref,
            dst_ref=up_dst,
            send_sem=sems.at[2],
            recv_sem=sems.at[3],
            device_id={"dp": other},
            device_id_type=MESH,
        ),
        pltpu.make_async_copy(down_ref, down_dst, sems.at[4]),
        pltpu.make_async_copy(up_ref, up_dst, sems.at[5]),
    ]
    for copy in copies:
        copy.start()
    for copy in copies:
        copy.wait()


def dp_gather(down, up):
    count = lax.axis_size("dp")
    return pl.pallas_call(
        _dp_gather_kernel,
        out_shape=(
            jax.ShapeDtypeStruct((down.shape[0], down.shape[1] * count), down.dtype),
            jax.ShapeDtypeStruct((up.shape[0] * count, up.shape[1]), up.dtype),
        ),
        in_specs=[pl.BlockSpec(memory_space=pltpu.VMEM)] * 2,
        out_specs=(pl.BlockSpec(memory_space=pl.ANY), pl.BlockSpec(memory_space=pl.ANY)),
        scratch_shapes=[pltpu.SemaphoreType.DMA((6,))],
        compiler_params=pltpu.CompilerParams(collective_id=5, has_side_effects=True),
    )(down, up)


def on_device(
    tokens,
    cotangent,
    expert_ids,
    slot_ids,
    gate_weights,
    latent_down,
    latent_up,
    expert_gate,
    expert_linear,
    expert_out,
):
    row_count = tokens.shape[0]
    pick_count = expert_ids.shape[1]
    local_count = expert_gate.shape[0]
    group_count = lax.axis_size("expert")
    expert_count = group_count * local_count
    capacity = min(
        row_count, 2 * ((9 * row_count * pick_count + 16 * expert_count - 1) // (16 * expert_count))
    )
    down_full, up_full = dp_gather(latent_down, latent_up)
    gate_full, linear_full, output_full = (
        lax.all_gather(expert_gate, "dp", axis=1, tiled=True),
        lax.all_gather(expert_linear, "dp", axis=1, tiled=True),
        lax.all_gather(expert_out, "dp", axis=2, tiled=True),
    )
    latent_part = jnp.dot(tokens, down_full, preferred_element_type=jnp.float32)
    back_part = lax.dot_general(
        cotangent, up_full, (((1,), (1,)), ((), ())), preferred_element_type=jnp.float32
    )
    width = latent_part.shape[1]
    both = pair_sum(jnp.concatenate([latent_part, back_part], axis=1), 1)
    latent = both[:, :width].astype(jnp.bfloat16)
    back_latent = both[:, width:]
    half_cap = capacity // 2
    side = lax.axis_index("half")
    swap = [(0, 1), (1, 0)]
    flat_slot = (expert_ids * capacity + slot_ids).reshape(-1)
    owned_shape = (expert_count, half_cap)
    owned_slot = (
        lax.broadcasted_iota(jnp.int32, owned_shape, 0) * capacity
        + side * half_cap
        + lax.broadcasted_iota(jnp.int32, owned_shape, 1)
    ).reshape(-1)
    matches = (flat_slot[None, :] == owned_slot[:, None]).reshape(-1, row_count, pick_count)
    picks = jnp.any(matches, axis=2).astype(jnp.bfloat16)
    weights = jnp.sum(jnp.where(matches, gate_weights[None], 0.0), axis=2)
    send_latent = jnp.dot(picks, latent, preferred_element_type=jnp.float32).astype(jnp.bfloat16)
    send_back = jnp.dot(
        weights,
        back_latent,
        precision=lax.Precision.HIGHEST,
        preferred_element_type=jnp.float32,
    ).astype(jnp.bfloat16)
    block_shape = (group_count, local_count, half_cap, width)
    mine_latent = all_to_all_kernel(send_latent.reshape(block_shape), 3, True)
    theirs_latent = lax.ppermute(mine_latent, "half", swap)
    mine_back = all_to_all_kernel(send_back.reshape(block_shape), 6, True)
    theirs_back = lax.ppermute(mine_back, "half", swap)
    mine = (mine_latent.reshape(block_shape), mine_back.reshape(block_shape))
    theirs = (theirs_latent.reshape(block_shape), theirs_back.reshape(block_shape))

    def forward(rows):
        rows_latent, rows_back = rows
        pre_gate = jnp.einsum(
            "neci,eih->nech", rows_latent, gate_full, preferred_element_type=jnp.float32
        )
        pre_linear = jnp.einsum(
            "neci,eih->nech", rows_latent, linear_full, preferred_element_type=jnp.float32
        )
        grad_hidden = jnp.einsum(
            "necj,ehj->nech", rows_back, output_full, preferred_element_type=jnp.float32
        )
        logistic = jax.nn.sigmoid(pre_gate)
        hidden = (pre_gate * logistic * pre_linear).astype(jnp.bfloat16)
        gate_delta = (
            grad_hidden * pre_linear * logistic * (1.0 + pre_gate * (1.0 - logistic))
        ).astype(jnp.bfloat16)
        linear_delta = (grad_hidden * pre_gate * logistic).astype(jnp.bfloat16)
        return rows_latent, rows_back, hidden, gate_delta, linear_delta

    def row_grad(gate_delta, linear_delta):
        row_part = jnp.einsum(
            "nech,eih->neci", gate_delta, gate_full, preferred_element_type=jnp.float32
        )
        return row_part + jnp.einsum(
            "nech,eih->neci", linear_delta, linear_full, preferred_element_type=jnp.float32
        )

    def weight_grads(rows_latent, rows_back, hidden, gate_delta, linear_delta):
        gate_part = jnp.einsum(
            "neci,nech->eih", rows_latent, gate_delta, preferred_element_type=jnp.float32
        )
        linear_part = jnp.einsum(
            "neci,nech->eih", rows_latent, linear_delta, preferred_element_type=jnp.float32
        )
        out_part = jnp.einsum(
            "nech,necj->ehj", hidden, rows_back, preferred_element_type=jnp.float32
        )
        return gate_part, linear_part, out_part

    own = forward(mine)
    own_row = row_grad(own[3], own[4])
    own_parts = weight_grads(*own)
    theirs, own_row, own_parts = lax.optimization_barrier((theirs, own_row, own_parts))
    other = forward(theirs)
    send_rows = row_grad(other[3], other[4]).astype(jnp.bfloat16)
    send_rows, other = lax.optimization_barrier((send_rows, other))
    other_rows = lax.ppermute(send_rows, "half", swap)
    other_parts = weight_grads(*other)
    parts = tuple((a + b).astype(jnp.bfloat16) for a, b in zip(own_parts, other_parts))
    other_rows, parts = lax.optimization_barrier((other_rows, parts))
    own_rows = own_row + other_rows.astype(jnp.float32)
    gate_part, linear_part, out_part = parts
    gate_share, linear_share, out_share = (
        lax.psum_scatter(
            gate_part.astype(jnp.bfloat16), "dp", scatter_dimension=1, tiled=True
        ).astype(jnp.float32),
        lax.psum_scatter(
            linear_part.astype(jnp.bfloat16), "dp", scatter_dimension=1, tiled=True
        ).astype(jnp.float32),
        lax.psum_scatter(
            out_part.astype(jnp.bfloat16), "dp", scatter_dimension=2, tiled=True
        ).astype(jnp.float32),
    )
    returned = all_to_all_kernel(own_rows.astype(jnp.bfloat16), 4)
    slot_rel = slot_ids - side * half_cap
    owned = (slot_rel >= 0) & (slot_rel < half_cap)
    position = jnp.where(owned, expert_ids * half_cap + slot_rel, -1).reshape(-1)
    slot_index = lax.broadcasted_iota(jnp.int32, (row_count * pick_count, expert_count * half_cap), 1)
    combine = (position[:, None] == slot_index).reshape(row_count, pick_count, -1)
    combine = jnp.any(combine, axis=1).astype(jnp.bfloat16)
    latent_half = jnp.dot(
        combine,
        returned.reshape(expert_count * half_cap, width),
        preferred_element_type=jnp.float32,
    )
    latent_grad = pair_sum(latent_half, 2)
    token_grad = lax.dot_general(
        latent_grad.astype(jnp.bfloat16),
        down_full,
        (((1,), (1,)), ((), ())),
        preferred_element_type=jnp.float32,
    )
    return (
        token_grad.astype(jnp.bfloat16),
        gate_share.astype(jnp.bfloat16),
        linear_share.astype(jnp.bfloat16),
        out_share.astype(jnp.bfloat16),
    )


def solution(mesh):
    in_specs = (
        P(("expert", "dp"), "half"),
        P(("expert", "dp"), "half"),
        P(("expert", "dp"), None),
        P(("expert", "dp"), None),
        P(("expert", "dp"), None),
        P("half", "dp"),
        P("dp", "half"),
        P("expert", "dp", "half"),
        P("expert", "dp", "half"),
        P("expert", "half", "dp"),
    )
    out_specs = (
        P(("expert", "dp"), "half"),
        P("expert", "dp", "half"),
        P("expert", "dp", "half"),
        P("expert", "half", "dp"),
    )
    return jax.shard_map(
        on_device, mesh=mesh, in_specs=in_specs, out_specs=out_specs, check_vma=False
    )
```

```python
import functools

import jax
import jax.numpy as jnp
from jax import lax
from jax.experimental import pallas as pl
from jax.experimental.pallas import tpu as pltpu
from jax.sharding import PartitionSpec as P

MESH = pl.DeviceIdType.MESH


def _pair_sum_kernel(x_ref, o_ref, buf, send_sem, recv_sem):
    other = 1 - lax.axis_index("half")
    barrier = pltpu.get_barrier_semaphore()
    pl.semaphore_signal(barrier, inc=1, device_id={"half": other}, device_id_type=MESH)
    pl.semaphore_wait(barrier, 1)
    copy = pltpu.make_async_remote_copy(
        src_ref=x_ref,
        dst_ref=buf,
        send_sem=send_sem,
        recv_sem=recv_sem,
        device_id={"half": other},
        device_id_type=MESH,
    )
    copy.start()
    copy.wait()
    o_ref[...] = x_ref[...].astype(jnp.float32) + buf[...].astype(jnp.float32)


def pair_sum(x, collective_id):
    x = x.astype(jnp.bfloat16)
    return pl.pallas_call(
        _pair_sum_kernel,
        out_shape=jax.ShapeDtypeStruct(x.shape, jnp.float32),
        in_specs=[pl.BlockSpec(memory_space=pltpu.VMEM)],
        out_specs=pl.BlockSpec(memory_space=pltpu.VMEM),
        scratch_shapes=[
            pltpu.VMEM(x.shape, x.dtype),
            pltpu.SemaphoreType.DMA(()),
            pltpu.SemaphoreType.DMA(()),
        ],
        compiler_params=pltpu.CompilerParams(collective_id=collective_id, has_side_effects=True),
    )(x)


def _all_to_all_kernel(x_ref, o_ref, send_sem, recv_sem, local_sem):
    count = x_ref.shape[0]
    me = lax.axis_index("expert")
    barrier = pltpu.get_barrier_semaphore()

    def greet(step, carry):
        peer = lax.rem(me + step, count)
        pl.semaphore_signal(barrier, inc=1, device_id={"expert": peer}, device_id_type=MESH)
        return carry

    lax.fori_loop(1, count, greet, 0)
    pl.semaphore_wait(barrier, count - 1)
    local = pltpu.make_async_copy(x_ref.at[me], o_ref.at[me], local_sem)
    local.start()

    def remote(peer):
        return pltpu.make_async_remote_copy(
            src_ref=x_ref.at[peer],
            dst_ref=o_ref.at[me],
            send_sem=send_sem.at[peer],
            recv_sem=recv_sem.at[me],
            device_id={"expert": peer},
            device_id_type=MESH,
        )

    def send(step, carry):
        remote(lax.rem(me + step, count)).start()
        return carry

    lax.fori_loop(1, count, send, 0)

    def drain(step, carry):
        peer = lax.rem(me + step, count)
        remote(peer).wait_send()
        pltpu.make_async_remote_copy(
            src_ref=x_ref.at[peer],
            dst_ref=o_ref.at[peer],
            send_sem=send_sem.at[peer],
            recv_sem=recv_sem.at[peer],
            device_id={"expert": peer},
            device_id_type=MESH,
        ).wait_recv()
        return carry

    lax.fori_loop(1, count, drain, 0)
    local.wait()


def all_to_all_kernel(x, collective_id, keep_blocks=False):
    count = lax.axis_size("expert")
    shape = x.shape
    blocks = x.reshape(count, -1, 128)
    out = pl.pallas_call(
        _all_to_all_kernel,
        out_shape=jax.ShapeDtypeStruct(blocks.shape, blocks.dtype),
        in_specs=[pl.BlockSpec(memory_space=pl.ANY)],
        out_specs=pl.BlockSpec(memory_space=pl.ANY),
        scratch_shapes=[
            pltpu.SemaphoreType.DMA((count,)),
            pltpu.SemaphoreType.DMA((count,)),
            pltpu.SemaphoreType.DMA(()),
        ],
        compiler_params=pltpu.CompilerParams(collective_id=collective_id, has_side_effects=True),
    )(blocks)
    return out if keep_blocks else out.reshape(shape)


def _dp_gather_kernel(down_ref, up_ref, down_out, up_out, sems):
    me = lax.axis_index("dp")
    other = 1 - me
    barrier = pltpu.get_barrier_semaphore()
    pl.semaphore_signal(barrier, inc=1, device_id={"dp": other}, device_id_type=MESH)
    pl.semaphore_wait(barrier, 1)
    cols = down_ref.shape[1]
    rows = up_ref.shape[0]
    down_dst = down_out.at[:, pl.ds(pl.multiple_of(me * cols, cols), cols)]
    up_dst = up_out.at[pl.ds(pl.multiple_of(me * rows, rows), rows), :]
    copies = [
        pltpu.make_async_remote_copy(
            src_ref=down_ref,
            dst_ref=down_dst,
            send_sem=sems.at[0],
            recv_sem=sems.at[1],
            device_id={"dp": other},
            device_id_type=MESH,
        ),
        pltpu.make_async_remote_copy(
            src_ref=up_ref,
            dst_ref=up_dst,
            send_sem=sems.at[2],
            recv_sem=sems.at[3],
            device_id={"dp": other},
            device_id_type=MESH,
        ),
        pltpu.make_async_copy(down_ref, down_dst, sems.at[4]),
        pltpu.make_async_copy(up_ref, up_dst, sems.at[5]),
    ]
    for copy in copies:
        copy.start()
    for copy in copies:
        copy.wait()


def dp_gather(down, up):
    count = lax.axis_size("dp")
    return pl.pallas_call(
        _dp_gather_kernel,
        out_shape=(
            jax.ShapeDtypeStruct((down.shape[0], down.shape[1] * count), down.dtype),
            jax.ShapeDtypeStruct((up.shape[0] * count, up.shape[1]), up.dtype),
        ),
        in_specs=[pl.BlockSpec(memory_space=pltpu.VMEM)] * 2,
        out_specs=(pl.BlockSpec(memory_space=pl.ANY), pl.BlockSpec(memory_space=pl.ANY)),
        scratch_shapes=[pltpu.SemaphoreType.DMA((6,))],
        compiler_params=pltpu.CompilerParams(collective_id=5, has_side_effects=True),
    )(down, up)


def on_device(
    tokens,
    cotangent,
    expert_ids,
    slot_ids,
    gate_weights,
    latent_down,
    latent_up,
    expert_gate,
    expert_linear,
    expert_out,
):
    row_count = tokens.shape[0]
    pick_count = expert_ids.shape[1]
    local_count = expert_gate.shape[0]
    group_count = lax.axis_size("expert")
    expert_count = group_count * local_count
    capacity = min(
        row_count, 2 * ((9 * row_count * pick_count + 16 * expert_count - 1) // (16 * expert_count))
    )
    down_full, up_full = dp_gather(latent_down, latent_up)
    gate_full, linear_full, output_full = (
        lax.all_gather(expert_gate, "dp", axis=1, tiled=True),
        lax.all_gather(expert_linear, "dp", axis=1, tiled=True),
        lax.all_gather(expert_out, "dp", axis=2, tiled=True),
    )
    latent_part = jnp.dot(tokens, down_full, preferred_element_type=jnp.float32)
    back_part = lax.dot_general(
        cotangent, up_full, (((1,), (1,)), ((), ())), preferred_element_type=jnp.float32
    )
    width = latent_part.shape[1]
    both = pair_sum(jnp.concatenate([latent_part, back_part], axis=1), 1)
    latent = both[:, :width].astype(jnp.bfloat16)
    back_latent = both[:, width:]
    half_cap = capacity // 2
    side = lax.axis_index("half")
    swap = [(0, 1), (1, 0)]
    flat_slot = (expert_ids * capacity + slot_ids).reshape(-1)
    owned_shape = (expert_count, half_cap)
    owned_slot = (
        lax.broadcasted_iota(jnp.int32, owned_shape, 0) * capacity
        + side * half_cap
        + lax.broadcasted_iota(jnp.int32, owned_shape, 1)
    ).reshape(-1)
    matches = (flat_slot[None, :] == owned_slot[:, None]).reshape(-1, row_count, pick_count)
    picks = jnp.any(matches, axis=2).astype(jnp.bfloat16)
    weights = jnp.sum(jnp.where(matches, gate_weights[None], 0.0), axis=2)
    send_latent = jnp.dot(picks, latent, preferred_element_type=jnp.float32).astype(jnp.bfloat16)
    send_back = jnp.dot(
        weights,
        back_latent,
        precision=lax.Precision.HIGHEST,
        preferred_element_type=jnp.float32,
    ).astype(jnp.bfloat16)
    block_shape = (group_count, local_count, half_cap, width)
    mine_latent = all_to_all_kernel(send_latent.reshape(block_shape), 3)
    theirs_latent = lax.ppermute(mine_latent, "half", swap)
    mine_back = all_to_all_kernel(send_back.reshape(block_shape), 6)
    theirs_back = lax.ppermute(mine_back, "half", swap)
    mine = (mine_latent, mine_back)
    theirs = (theirs_latent, theirs_back)

    def forward(rows):
        rows_latent, rows_back = rows
        pre_gate = jnp.einsum(
            "neci,eih->nech", rows_latent, gate_full, preferred_element_type=jnp.float32
        )
        pre_linear = jnp.einsum(
            "neci,eih->nech", rows_latent, linear_full, preferred_element_type=jnp.float32
        )
        grad_hidden = jnp.einsum(
            "necj,ehj->nech", rows_back, output_full, preferred_element_type=jnp.float32
        )
        logistic = jax.nn.sigmoid(pre_gate)
        hidden = (pre_gate * logistic * pre_linear).astype(jnp.bfloat16)
        gate_delta = (
            grad_hidden * pre_linear * logistic * (1.0 + pre_gate * (1.0 - logistic))
        ).astype(jnp.bfloat16)
        linear_delta = (grad_hidden * pre_gate * logistic).astype(jnp.bfloat16)
        return rows_latent, rows_back, hidden, gate_delta, linear_delta

    def row_grad(gate_delta, linear_delta):
        row_part = jnp.einsum(
            "nech,eih->neci", gate_delta, gate_full, preferred_element_type=jnp.float32
        )
        return row_part + jnp.einsum(
            "nech,eih->neci", linear_delta, linear_full, preferred_element_type=jnp.float32
        )

    def weight_grads(rows_latent, rows_back, hidden, gate_delta, linear_delta):
        gate_part = jnp.einsum(
            "neci,nech->eih", rows_latent, gate_delta, preferred_element_type=jnp.float32
        )
        linear_part = jnp.einsum(
            "neci,nech->eih", rows_latent, linear_delta, preferred_element_type=jnp.float32
        )
        out_part = jnp.einsum(
            "nech,necj->ehj", hidden, rows_back, preferred_element_type=jnp.float32
        )
        return gate_part, linear_part, out_part

    own = forward(mine)
    own_row = row_grad(own[3], own[4])
    own_parts = weight_grads(*own)
    theirs, own_row, own_parts = lax.optimization_barrier((theirs, own_row, own_parts))
    other = forward(theirs)
    send_rows = row_grad(other[3], other[4]).astype(jnp.bfloat16)
    send_rows, other = lax.optimization_barrier((send_rows, other))
    other_rows = lax.ppermute(send_rows, "half", swap)
    other_parts = weight_grads(*other)
    parts = tuple((a + b).astype(jnp.bfloat16) for a, b in zip(own_parts, other_parts))
    other_rows, parts = lax.optimization_barrier((other_rows, parts))
    own_rows = own_row + other_rows.astype(jnp.float32)
    gate_part, linear_part, out_part = parts
    gate_share, linear_share, out_share = (
        lax.psum_scatter(
            gate_part.astype(jnp.bfloat16), "dp", scatter_dimension=1, tiled=True
        ).astype(jnp.float32),
        lax.psum_scatter(
            linear_part.astype(jnp.bfloat16), "dp", scatter_dimension=1, tiled=True
        ).astype(jnp.float32),
        lax.psum_scatter(
            out_part.astype(jnp.bfloat16), "dp", scatter_dimension=2, tiled=True
        ).astype(jnp.float32),
    )
    returned = all_to_all_kernel(own_rows.astype(jnp.bfloat16), 4, True)
    slot_rel = slot_ids - side * half_cap
    owned = (slot_rel >= 0) & (slot_rel < half_cap)
    position = jnp.where(owned, expert_ids * half_cap + slot_rel, -1).reshape(-1)
    slot_index = lax.broadcasted_iota(jnp.int32, (row_count * pick_count, expert_count * half_cap), 1)
    combine = (position[:, None] == slot_index).reshape(row_count, pick_count, -1)
    combine = jnp.any(combine, axis=1).astype(jnp.bfloat16)
    lanes = returned.shape[-1]
    latent_half = jnp.einsum(
        "tec,ecjk->tjk",
        combine.reshape(row_count, expert_count, half_cap),
        returned.reshape(expert_count, half_cap, width // lanes, lanes),
        preferred_element_type=jnp.float32,
    ).reshape(row_count, width)
    latent_grad = pair_sum(latent_half, 2)
    token_grad = lax.dot_general(
        latent_grad.astype(jnp.bfloat16),
        down_full,
        (((1,), (1,)), ((), ())),
        preferred_element_type=jnp.float32,
    )
    return (
        token_grad.astype(jnp.bfloat16),
        gate_share.astype(jnp.bfloat16),
        linear_share.astype(jnp.bfloat16),
        out_share.astype(jnp.bfloat16),
    )


def solution(mesh):
    in_specs = (
        P(("expert", "dp"), "half"),
        P(("expert", "dp"), "half"),
        P(("expert", "dp"), None),
        P(("expert", "dp"), None),
        P(("expert", "dp"), None),
        P("half", "dp"),
        P("dp", "half"),
        P("expert", "dp", "half"),
        P("expert", "dp", "half"),
        P("expert", "half", "dp"),
    )
    out_specs = (
        P(("expert", "dp"), "half"),
        P("expert", "dp", "half"),
        P("expert", "dp", "half"),
        P("expert", "half", "dp"),
    )
    return jax.shard_map(
        on_device, mesh=mesh, in_specs=in_specs, out_specs=out_specs, check_vma=False
    )
```
